512 devices in a mesh: seq: 128 (over x, y_hi, z), fsdp: 4 (over y_lo, core).
Axes of the slice: x: 4, y: 4 (y_hi: 2, y_lo: 2; y = y_hi * 2 + y_lo), z: 16, core: 2. Of those that a mesh axis runs over, the one named last changes fastest.
Arguments:
- block_input: bfloat16 [8, 16384, 1536], P('fsdp', 'seq'), may hold values from -6 to 6
- dilated_weight: bfloat16 [3, 1536, 768], P(None, 'fsdp'), may hold values from -0.09375 to 0.09375
- w_project: bfloat16 [768, 1536], P('fsdp'), may hold values from -0.21875 to 0.21875
- gain_first: float32 [1536], replicated, may hold values from 0.5 to 1.5
- gain_second: float32 [768], replicated, may hold values from 0.5 to 1.5
- grad_output: bfloat16 [8, 16384, 1536], P('fsdp', 'seq'), may hold values from -6 to 6
Outputs:
- grad_input: bfloat16 [8, 16384, 1536], P('fsdp', 'seq')
- grad_gain_first: float32 [1536], replicated
- grad_gain_second: float32 [768], replicated
The draws below stay inside these ranges and needn't reach their ends.
All inputs are finite; a program needn't handle non-finite values.
Results may differ from the reference program's by a relative error of at most 0.008.
Values may be sent and summed in bfloat16 or wider, within the bound.
No kernel may reach another device: no remote copies, remote signals or barrier semaphores. Data moves between devices by JAX's collectives and lax.ppermute only.
A program may use at most 64 MiB of HBM per device.

```python
import jax
import jax.numpy as jnp
from jax import lax

C = 1536
H = 768
BATCH = 8
BINS = 16384
DILATION_STEP = 2048


def steps_of(own_key, dims, cuts, least, top_value):
    factor_of, own = 1.0, jax.random.fold_in(own_key, 6)
    for dim, blocks in cuts:
        heights = jnp.exp(jax.random.uniform(jax.random.fold_in(own, dim), (blocks,), jnp.float32, least / len(cuts), top_value / len(cuts)))
        factor_of = factor_of * jnp.repeat(heights, dims[dim] // blocks).reshape([-1 if axis == dim else 1 for axis in range(len(dims))])
    return factor_of


def noise(key, shape, deviation, bound, shards=(), held_as=jnp.bfloat16):
    values = jax.random.normal(key, shape, jnp.float32) * deviation
    if len(shards) > 0:
        values = steps_of(key, shape, shards, -0.22, 0.18) * values
    return jnp.clip(values, min=-bound, max=bound).astype(held_as)


def setup_inputs(seed: int = 0) -> dict:
    keys = jax.random.split(jax.random.key(seed), 7)
    return {
        "block_input": noise(keys[0], (BATCH, BINS, C), 1.0, 6.0, ((0, 4), (1, 128))),
        "dilated_weight": noise(keys[1], (3, C, H), (3 * C) ** -0.5, 0.09375, ((1, 4),)),
        "w_project": noise(keys[2], (H, C), H ** -0.5, 0.21875, ((0, 4),)),
        "gain_first": jnp.clip(1.0 + 0.1 * jax.random.normal(keys[3], (C,), jnp.float32), 0.5, 1.5),
        "gain_second": jnp.clip(1.0 + 0.1 * jax.random.normal(keys[4], (H,), jnp.float32), 0.5, 1.5),
        "grad_output": noise(keys[5], (BATCH, BINS, C), 1.0, 6.0, ((0, 4), (1, 128))),
    }


def norm_act(values, factor):
    centre = values - lax.optimization_barrier(jnp.mean(values, axis=-1, keepdims=True))
    spread = lax.optimization_barrier(jnp.mean(centre * centre, axis=-1, keepdims=True))
    return jax.nn.gelu(centre * lax.rsqrt(spread + 1e-05) * factor)

def displace_rows(values, amount):
    if amount > 0:
        return jnp.concatenate([jnp.zeros_like(values[:amount]), values[:-amount]], axis=0)
    return jnp.concatenate([values[-amount:], jnp.zeros_like(values[:-amount])], axis=0)

def reference(block_input, dilated_weight, w_project, gain_first, gain_second, grad_output):

    def per_sample(sample):
        inputs, cotangent = sample
        widened = inputs.astype(jnp.float32)
        hidden_state = norm_act(widened, gain_first).astype(jnp.bfloat16)
        mixed_state = jnp.dot(displace_rows(hidden_state, DILATION_STEP), dilated_weight[0], preferred_element_type=jnp.float32)
        mixed_state = mixed_state + jnp.dot(hidden_state, dilated_weight[1], preferred_element_type=jnp.float32)
        mixed_state = mixed_state + jnp.dot(displace_rows(hidden_state, -DILATION_STEP), dilated_weight[2], preferred_element_type=jnp.float32)
        mixed_state = mixed_state.astype(jnp.bfloat16)
        grad_hidden2 = jnp.dot(cotangent, w_project.T, preferred_element_type=jnp.float32)
        unused, pull_second = jax.vjp(norm_act, mixed_state.astype(jnp.float32), gain_second)
        mixed_gradient, grad_second = pull_second(grad_hidden2)
        mixed_gradient = mixed_gradient.astype(jnp.bfloat16)
        hidden_gradient = jnp.dot(displace_rows(mixed_gradient, -DILATION_STEP), dilated_weight[0].T, preferred_element_type=jnp.float32)
        hidden_gradient = hidden_gradient + jnp.dot(mixed_gradient, dilated_weight[1].T, preferred_element_type=jnp.float32)
        hidden_gradient = hidden_gradient + jnp.dot(displace_rows(mixed_gradient, DILATION_STEP), dilated_weight[2].T, preferred_element_type=jnp.float32)
        unused2, pull_first = jax.vjp(norm_act, widened, gain_first)
        grad_branch, grad_first = pull_first(hidden_gradient)
        grad_in = (cotangent.astype(jnp.float32) + grad_branch).astype(jnp.bfloat16)
        return (grad_in, grad_first, grad_second)
    grad_input, first_terms, second_terms = lax.map(per_sample, (block_input, grad_output))
    return (grad_input, lax.optimization_barrier(jnp.sum(first_terms, axis=0)), lax.optimization_barrier(jnp.sum(second_terms, axis=0)))
```

```python
import jax
import jax.numpy as jnp
import numpy as np
from jax import lax
from jax.sharding import Mesh
from jax.sharding import PartitionSpec as P

AXES = ("x", "yh", "z", "yl", "c")
SIZES = (4, 2, 16, 2, 2)
SEQ = ("x", "yh", "z")
FSDP = ("yl", "c")


def permute(value, target):
    pairs = []
    for place in np.ndindex(*SIZES):
        to = target(*place)
        if to is not None:
            pairs.append(
                (int(np.ravel_multi_index(place, SIZES)), int(np.ravel_multi_index(to, SIZES)))
            )
    return lax.ppermute(value, AXES, pairs)


def along_y(steps):
    def target(x, yh, z, yl, c):
        y = (2 * yh + yl + steps) % 4
        return (x, y // 2, z, y % 2, c)

    return target


def sister(x, yh, z, yl, c):
    return (x, yh, z, yl, 1 - c)


def along_bins(steps):
    def target(x, yh, z, yl, c):
        k = 2 * x + yh + steps
        return (k // 2, k % 2, z, yl, c) if 0 <= k < 8 else None

    return target


def total(value, axes):
    count = lax.axis_size(axes)
    copies = lax.optimization_barrier(jnp.broadcast_to(value[None], (count,) + value.shape))
    return jnp.sum(lax.all_to_all(copies, axes, 0, 0), axis=0)


def norm_act(values, factor):
    centre = values - jnp.mean(values, axis=-1, keepdims=True)
    spread = jnp.mean(centre * centre, axis=-1, keepdims=True)
    return jax.nn.gelu(centre * lax.rsqrt(spread + 1e-05) * factor)


def dot(a, b):
    return lax.dot_general(a, b, (((1,), (0,)), ((), ())), preferred_element_type=jnp.float32)


def dot_t(a, b):
    return lax.dot_general(a, b, (((1,), (1,)), ((), ())), preferred_element_type=jnp.float32)


def body(block_input, weight, project, gain_first, gain_second, grad_output):
    samples, bins, channels = block_input.shape
    rows = samples * bins
    part = weight.shape[1]
    part_h = project.shape[0]
    inputs = block_input.reshape(rows, channels)
    cotangent = grad_output.reshape(rows, channels)

    own = lax.axis_index(FSDP)
    order = [own, own ^ 1, own ^ 2, own ^ 3]

    w_up = permute(weight[:, : part // 2], along_y(1))
    w_down = permute(weight[:, part // 2 :], along_y(-1))
    w_sister = permute(weight, sister)
    p_up = permute(project[: part_h // 2], along_y(1))
    p_down = permute(project[part_h // 2 :], along_y(-1))
    p_sister = permute(project, sister)
    w_all = jnp.concatenate(
        [weight, w_sister, w_up, w_down, permute(w_up, sister), permute(w_down, sister)], axis=1
    )
    p_all = jnp.concatenate(
        [project, p_sister, p_up, p_down, permute(p_up, sister), permute(p_down, sister)], axis=0
    )

    def reorder(value, width):
        return jnp.concatenate(
            [lax.dynamic_slice_in_dim(value, f * width, width, axis=1) for f in order], axis=1
        )

    widened = inputs.astype(jnp.float32)
    hidden = norm_act(widened, gain_first).astype(jnp.bfloat16)
    hidden = reorder(hidden, part)
    lagging = permute(hidden, along_bins(1))
    leading = permute(hidden, along_bins(-1))
    mixed = dot(lagging, w_all[0]) + dot(hidden, w_all[1]) + dot(leading, w_all[2])
    mixed = mixed.astype(jnp.bfloat16)
    grad_hidden2 = reorder(dot_t(cotangent, p_all), part_h)
    unused, pull_second = jax.vjp(norm_act, mixed.astype(jnp.float32), gain_second)
    grad_mixed, second = pull_second(grad_hidden2)
    grad_mixed = grad_mixed.astype(jnp.bfloat16)
    ahead = permute(grad_mixed, along_bins(-1))
    behind = permute(grad_mixed, along_bins(1))
    grad_hidden = dot_t(ahead, w_all[0]) + dot_t(grad_mixed, w_all[1]) + dot_t(behind, w_all[2])
    grad_hidden = reorder(grad_hidden, part)
    unused2, pull_first = jax.vjp(norm_act, widened, gain_first)
    grad_branch, first = pull_first(grad_hidden)
    grad_input = (cotangent.astype(jnp.float32) + grad_branch).astype(jnp.bfloat16)

    sums = jnp.concatenate([first, second]).reshape(-1, 128)
    sums = total(total(sums, ("x", "yh", "yl", "c")), "z").reshape(-1)
    return (grad_input.reshape(block_input.shape), sums[:channels], sums[channels:])


def solution(mesh):
    fine = Mesh(mesh.devices.reshape(SIZES), AXES)
    in_specs = (
        P(FSDP, SEQ, None),
        P(None, FSDP, None),
        P(FSDP, None),
        P(),
        P(),
        P(FSDP, SEQ, None),
    )
    out_specs = (P(FSDP, SEQ, None), P(), P())
    return jax.shard_map(body, mesh=fine, in_specs=in_specs, out_specs=out_specs, check_vma=False)
```

```python
import jax
import jax.numpy as jnp
import numpy as np
from jax import lax
from jax.sharding import Mesh
from jax.sharding import PartitionSpec as P

AXES = ("x", "yh", "z", "yl", "c")
SIZES = (4, 2, 16, 2, 2)
SEQ = ("x", "yh", "z")
FSDP = ("yl", "c")
HALF = 0.7978845608028654


def permute(value, target):
    pairs = []
    for place in np.ndindex(*SIZES):
        to = target(*place)
        if to is not None:
            pairs.append(
                (int(np.ravel_multi_index(place, SIZES)), int(np.ravel_multi_index(to, SIZES)))
            )
    return lax.ppermute(value, AXES, pairs)


def along_y(steps):
    def target(x, yh, z, yl, c):
        y = (2 * yh + yl + steps) % 4
        return (x, y // 2, z, y % 2, c)

    return target


def along_z(steps):
    def target(x, yh, z, yl, c):
        return (x, yh, (z + steps) % 16, yl, c)

    return target


def sister(x, yh, z, yl, c):
    return (x, yh, z, yl, 1 - c)


def along_bins(steps):
    def target(x, yh, z, yl, c):
        k = 2 * x + yh + steps
        return (k // 2, k % 2, z, yl, c) if 0 <= k < 8 else None

    return target


def total(value, axes):
    count = lax.axis_size(axes)
    copies = lax.optimization_barrier(jnp.broadcast_to(value[None], (count,) + value.shape))
    return jnp.sum(lax.all_to_all(copies, axes, 0, 0), axis=0)


def normed(values):
    centre = values - jnp.mean(values, axis=-1, keepdims=True)
    spread = jnp.mean(centre * centre, axis=-1, keepdims=True)
    scale = lax.rsqrt(spread + 1e-05)
    return centre * scale, scale


def act(a):
    return 0.5 * a * (1.0 + jnp.tanh(HALF * (a + 0.044715 * a * a * a)))


def slope(a):
    t = jnp.tanh(HALF * (a + 0.044715 * a * a * a))
    return 0.5 * (1.0 + t) + 0.5 * a * (1.0 - t * t) * (HALF * (1.0 + 0.134145 * a * a))


def norm_back(grad, scale, unit):
    return scale * (
        grad
        - jnp.mean(grad, axis=-1, keepdims=True)
        - unit * jnp.mean(grad * unit, axis=-1, keepdims=True)
    )


def dot(a, b):
    return lax.dot_general(a, b, (((1,), (0,)), ((), ())), preferred_element_type=jnp.float32)


def dot_t(a, b):
    return lax.dot_general(a, b, (((1,), (1,)), ((), ())), preferred_element_type=jnp.float32)


def body(block_input, weight, project, gain_first, gain_second, grad_output):
    samples, bins, channels = block_input.shape
    rows = samples * bins
    width = weight.shape[2]
    part = weight.shape[1]
    part_h = project.shape[0]
    inputs = block_input.reshape(rows, channels)
    cotangent = grad_output.reshape(rows, channels)

    own = lax.axis_index(FSDP)
    odd = lax.axis_index("z") % 2

    slabs = jnp.concatenate(
        [weight, jnp.concatenate([project[:, :width], project[:, width:]], axis=0)[None]], axis=0
    )
    up = permute(lax.dynamic_index_in_dim(slabs, 2 * odd, 0, False), along_y(1))
    down = permute(lax.dynamic_index_in_dim(slabs, 2 * odd + 1, 0, False), along_y(-1))
    lagging = permute(inputs, along_bins(1))
    leading = permute(inputs, along_bins(-1))
    slabs_s = permute(slabs, sister)
    up_z = permute(up, along_z(1))
    down_z = permute(down, along_z(-1))
    first = [up, down, up_z, down_z]
    second = [permute(piece, sister) for piece in first]

    def far(pieces, k):
        return jnp.where(odd == 0, pieces[k], pieces[k ^ 2])

    def full(k):
        whole = jnp.zeros((4 * part, width), jnp.bfloat16)
        for piece, f in (
            (slabs[k], own),
            (slabs_s[k], own ^ 1),
            (far(first, k), own ^ 2),
            (far(second, k), own ^ 3),
        ):
            whole = lax.dynamic_update_slice(whole, piece, (f * part, 0))
        return whole

    taps = [full(k) for k in range(3)]
    proj = full(3).reshape(4, 2, part_h, width)
    proj = [proj[:, j].reshape(4 * part_h, width) for j in range(2)]

    grad_hidden2 = dot_t(cotangent[:, :width], proj[0]) + dot_t(cotangent[:, width:], proj[1])

    units, scales, hiddens, weighs, slopes = [], [], [], [], []
    for block in (lagging, inputs, leading):
        unit, scale = normed(block.astype(jnp.float32))
        a = unit * gain_first
        units.append(unit)
        scales.append(scale)
        hiddens.append(act(a).astype(jnp.bfloat16))
        slopes.append(slope(a))
        weighs.append(slopes[-1] * unit)

    mixed = dot(hiddens[1], taps[1]) + dot(hiddens[0], taps[0]) + dot(hiddens[2], taps[2])
    mixed = mixed.astype(jnp.bfloat16).astype(jnp.float32)
    unit2, scale2 = normed(mixed)
    grad_a = grad_hidden2 * slope(unit2 * gain_second)
    second_sum = jnp.sum(grad_a * unit2, axis=0)
    grad_mixed = norm_back(grad_a * gain_second, scale2, unit2).astype(jnp.bfloat16)

    ahead = permute(grad_mixed, along_bins(-1))
    behind = permute(grad_mixed, along_bins(1))

    terms = [dot_t(grad_mixed, tap) for tap in taps]
    first_sum = jnp.sum(terms[0] * weighs[0] + terms[1] * weighs[1] + terms[2] * weighs[2], axis=0)
    sums = jnp.concatenate([first_sum, second_sum]).reshape(-1, 128)
    sums = total(sums, ("x", "yh", "yl", "c"))
    ahead, behind, sums = lax.optimization_barrier((ahead, behind, sums))
    sums = total(sums, "z").reshape(-1)

    grad_hidden = terms[1] + dot_t(ahead, taps[0]) + dot_t(behind, taps[2])
    grad_branch = norm_back(grad_hidden * slopes[1] * gain_first, scales[1], units[1])
    grad_input = (cotangent.astype(jnp.float32) + grad_branch).astype(jnp.bfloat16)
    return (grad_input.reshape(block_input.shape), sums[:channels], sums[channels:])


def solution(mesh):
    fine = Mesh(mesh.devices.reshape(SIZES), AXES)
    in_specs = (
        P(FSDP, SEQ, None),
        P(None, FSDP, None),
        P(FSDP, None),
        P(),
        P(),
        P(FSDP, SEQ, None),
    )
    out_specs = (P(FSDP, SEQ, None), P(), P())
    return jax.shard_map(body, mesh=fine, in_specs=in_specs, out_specs=out_specs, check_vma=False)
```

```python
import jax
import jax.numpy as jnp
import numpy as np
from jax import lax
from jax.experimental import pallas as pl
from jax.experimental.pallas import tpu as pltpu
from jax.sharding import Mesh
from jax.sharding import PartitionSpec as P

AXES = ("x", "yh", "z", "yl", "c")
SIZES = (4, 2, 16, 2, 2)
SEQ = ("x", "yh", "z")
FSDP = ("yl", "c")
HALF = 0.7978845608028654
VMEM_LIMIT = 32 * 1024 * 1024


def permute(value, target):
    pairs = []
    for place in np.ndindex(*SIZES):
        to = target(*place)
        if to is not None:
            pairs.append(
                (int(np.ravel_multi_index(place, SIZES)), int(np.ravel_multi_index(to, SIZES)))
            )
    return lax.ppermute(value, AXES, pairs)


def along_y(steps):
    def target(x, yh, z, yl, c):
        y = (2 * yh + yl + steps) % 4
        return (x, y // 2, z, y % 2, c)

    return target


def along_z(steps):
    def target(x, yh, z, yl, c):
        return (x, yh, (z + steps) % 16, yl, c)

    return target


def sister(x, yh, z, yl, c):
    return (x, yh, z, yl, 1 - c)


def along_bins(steps):
    def target(x, yh, z, yl, c):
        k = 2 * x + yh + steps
        return (k // 2, k % 2, z, yl, c) if 0 <= k < 8 else None

    return target


def total(value, axes):
    count = lax.axis_size(axes)
    copies = lax.optimization_barrier(jnp.broadcast_to(value[None], (count,) + value.shape))
    return jnp.sum(lax.all_to_all(copies, axes, 0, 0), axis=0)


CHUNK = 16


def normed(values):
    centre = values - jnp.mean(values, axis=-1, keepdims=True)
    spread = jnp.mean(centre * centre, axis=-1, keepdims=True)
    scale = lax.rsqrt(spread + 1e-05)
    return centre * scale, scale


def bend(a):
    square = a * a
    t = jnp.tanh(HALF * a * (1.0 + 0.044715 * square))
    return t, 0.5 * (1.0 + t) + (0.5 * HALF) * a * (1.0 - t * t) * (1.0 + 0.134145 * square)


def norm_back(grad, scale, unit):
    return scale * (
        grad
        - jnp.mean(grad, axis=-1, keepdims=True)
        - unit * jnp.mean(grad * unit, axis=-1, keepdims=True)
    )


def over_rows(count, step):
    def run(i, carry):
        step(pl.ds(pl.multiple_of(i * CHUNK, CHUNK), CHUNK))
        return carry

    lax.fori_loop(0, count // CHUNK, run, 0, unroll=True)


def prepare_kernel(block, gain, hidden, weigh):
    def step(rows):
        unit, scale = normed(block[rows, :].astype(jnp.float32))
        a = unit * gain[...]
        t, slope = bend(a)
        hidden[rows, :] = (0.5 * a * (1.0 + t)).astype(jnp.bfloat16)
        weigh[rows, :] = slope * unit

    over_rows(block.shape[0], step)


def middle_kernel(
    h0, h1, h2, e0, e1, e2, t0, t1, t2, grad2, gain, grad_mixed, first, second, mixed, partial
):
    rows, width = mixed.shape
    channels = e0.shape[1]
    for n in range(0, width, 256):
        cols = slice(n, n + 256)
        mixed[:, cols] = (
            dot(h1[...], t1[:, cols]) + dot(h0[...], t0[:, cols]) + dot(h2[...], t2[:, cols])
        )
    partial[...] = jnp.zeros_like(partial)

    def step(at):
        unit, scale = normed(mixed[at, :].astype(jnp.bfloat16).astype(jnp.float32))
        unused, slope = bend(unit * gain[...])
        grad_a = grad2[at, :] * slope
        terms = grad_a * unit
        partial[...] += jnp.sum(terms.reshape(-1, 8, width), axis=0)
        grad_mixed[at, :] = norm_back(grad_a * gain[...], scale, unit).astype(jnp.bfloat16)

    over_rows(rows, step)
    second[...] = jnp.sum(partial[...], axis=0, keepdims=True)
    for n in range(0, channels, 256):
        cols = slice(n, n + 256)
        terms = dot_t(grad_mixed[...], t0[cols, :]) * e0[:, cols]
        terms += dot_t(grad_mixed[...], t1[cols, :]) * e1[:, cols]
        terms += dot_t(grad_mixed[...], t2[cols, :]) * e2[:, cols]
        first[:, cols] = jnp.sum(terms, axis=0, keepdims=True)


def last_kernel(block, cotangent, ahead, here, behind, t0, t1, t2, gain, result, grads):
    rows, channels = block.shape
    for n in range(0, channels, 256):
        cols = slice(n, n + 256)
        grads[:, cols] = (
            dot_t(here[...], t1[cols, :])
            + dot_t(ahead[...], t0[cols, :])
            + dot_t(behind[...], t2[cols, :])
        )

    def step(at):
        unit, scale = normed(block[at, :].astype(jnp.float32))
        unused, slope = bend(unit * gain[...])
        branch = norm_back(grads[at, :] * slope * gain[...], scale, unit)
        result[at, :] = (cotangent[at, :].astype(jnp.float32) + branch).astype(jnp.bfloat16)

    over_rows(rows, step)


def call(kernel, name, out_shape, scratch, flops, *operands):
    moved = sum(v.size * v.dtype.itemsize for v in operands)
    return pl.pallas_call(
        kernel,
        name=name,
        out_shape=out_shape,
        in_specs=[pl.BlockSpec(memory_space=pltpu.VMEM)] * len(operands),
        out_specs=jax.tree.map(lambda _: pl.BlockSpec(memory_space=pltpu.VMEM), out_shape),
        scratch_shapes=scratch,
        cost_estimate=pl.CostEstimate(flops=flops, bytes_accessed=moved, transcendentals=0),
        compiler_params=pltpu.CompilerParams(vmem_limit_bytes=VMEM_LIMIT),
    )(*operands)


def dot(a, b):
    return lax.dot_general(a, b, (((1,), (0,)), ((), ())), preferred_element_type=jnp.float32)


def dot_t(a, b):
    return lax.dot_general(a, b, (((1,), (1,)), ((), ())), preferred_element_type=jnp.float32)


def body(block_input, weight, project, gain_first, gain_second, grad_output):
    samples, bins, channels = block_input.shape
    rows = samples * bins
    width = weight.shape[2]
    part = weight.shape[1]
    part_h = project.shape[0]
    inputs = block_input.reshape(rows, channels)
    cotangent = grad_output.reshape(rows, channels)

    own = lax.axis_index(FSDP)
    odd = lax.axis_index("z") % 2

    folded = jnp.concatenate([project[:, :width], project[:, width:]], axis=0)
    slabs = [weight[0], weight[1], weight[2], folded]
    near_u = jnp.where(odd == 0, slabs[0], slabs[2])
    near_d = jnp.where(odd == 0, slabs[1], slabs[3])
    weight_s = permute(weight, sister)
    up = permute(near_u, along_y(1))
    down = permute(near_d, along_y(-1))
    slabs_s = [weight_s[0], weight_s[1], weight_s[2], permute(folded, sister)]
    up_z = permute(up, along_z(1))
    down_z = permute(down, along_z(-1))
    first = [up, down, up_z, down_z]
    second = [permute(piece, sister) for piece in first]

    def far(pieces, k):
        return jnp.where(odd == 0, pieces[k], pieces[k ^ 2])

    def full(k):
        whole = jnp.zeros((4 * part, width), jnp.bfloat16)
        for piece, f in (
            (slabs[k], own),
            (slabs_s[k], own ^ 1),
            (far(first, k), own ^ 2),
            (far(second, k), own ^ 3),
        ):
            whole = lax.dynamic_update_slice(whole, piece, (f * part, 0))
        return whole

    taps = [full(k) for k in range(3)]
    proj = full(3).reshape(4, 2, part_h, width)
    proj = [proj[:, j].reshape(4 * part_h, width) for j in range(2)]

    grad_hidden2 = dot_t(cotangent[:, :width], proj[0]) + dot_t(cotangent[:, width:], proj[1])

    f32, bf16 = jnp.float32, jnp.bfloat16
    gain1, gain2 = gain_first[None], gain_second[None]

    def prepare(block):
        return call(
            prepare_kernel,
            "prepare",
            [jax.ShapeDtypeStruct(block.shape, bf16), jax.ShapeDtypeStruct(block.shape, f32)],
            [],
            40 * block.size,
            block,
            gain1,
        )

    own_pair = prepare(inputs)
    halo, own_pair = lax.optimization_barrier((inputs, own_pair))
    lagging = permute(halo, along_bins(1))
    leading = permute(halo, along_bins(-1))
    pairs = [prepare(lagging), own_pair, prepare(leading)]
    hiddens = [pair[0] for pair in pairs]
    weighs = [pair[1] for pair in pairs]

    work = 2 * rows * channels * width
    grad_mixed, first_sum, second_sum = call(
        middle_kernel,
        "middle",
        [
            jax.ShapeDtypeStruct((rows, width), bf16),
            jax.ShapeDtypeStruct((1, channels), f32),
            jax.ShapeDtypeStruct((1, width), f32),
        ],
        [pltpu.VMEM((rows, width), f32), pltpu.VMEM((8, width), f32)],
        6 * work,
        *hiddens,
        *weighs,
        *taps,
        grad_hidden2,
        gain2,
    )
    first_sum, second_sum = first_sum[0], second_sum[0]
    ahead = permute(grad_mixed, along_bins(-1))
    behind = permute(grad_mixed, along_bins(1))

    sums = jnp.concatenate([first_sum, second_sum]).reshape(-1, 128)
    sums = total(sums, ("x", "yh", "yl", "c"))
    ahead, behind, sums = lax.optimization_barrier((ahead, behind, sums))
    sums = total(sums, "z").reshape(-1)

    grad_input = call(
        last_kernel,
        "last",
        jax.ShapeDtypeStruct(inputs.shape, bf16),
        [pltpu.VMEM(inputs.shape, f32)],
        3 * work,
        inputs,
        cotangent,
        ahead,
        grad_mixed,
        behind,
        *taps,
        gain1,
    )
    return (grad_input.reshape(block_input.shape), sums[:channels], sums[channels:])


def solution(mesh):
    fine = Mesh(mesh.devices.reshape(SIZES), AXES)
    in_specs = (
        P(FSDP, SEQ, None),
        P(None, FSDP, None),
        P(FSDP, None),
        P(),
        P(),
        P(FSDP, SEQ, None),
    )
    out_specs = (P(FSDP, SEQ, None), P(), P())
    return jax.shard_map(body, mesh=fine, in_specs=in_specs, out_specs=out_specs, check_vma=False)
```

```python
import jax
import jax.numpy as jnp
import numpy as np
from jax import lax
from jax.experimental import pallas as pl
from jax.experimental.pallas import tpu as pltpu
from jax.sharding import Mesh
from jax.sharding import PartitionSpec as P

AXES = ("x", "yh", "z", "yl", "c")
SIZES = (4, 2, 16, 2, 2)
SEQ = ("x", "yh", "z")
FSDP = ("yl", "c")
HALF = 0.7978845608028654
VMEM_LIMIT = 32 * 1024 * 1024


def permute(value, target):
    pairs = []
    for place in np.ndindex(*SIZES):
        to = target(*place)
        if to is not None:
            pairs.append(
                (int(np.ravel_multi_index(place, SIZES)), int(np.ravel_multi_index(to, SIZES)))
            )
    return lax.ppermute(value, AXES, pairs)


def along_y(steps):
    def target(x, yh, z, yl, c):
        y = (2 * yh + yl + steps) % 4
        return (x, y // 2, z, y % 2, c)

    return target


def sister(x, yh, z, yl, c):
    return (x, yh, z, yl, 1 - c)


def along_bins(steps):
    def target(x, yh, z, yl, c):
        k = 2 * x + yh + steps
        return (k // 2, k % 2, z, yl, c) if 0 <= k < 8 else None

    return target


CHUNK = 16


def normed(values):
    centre = values - jnp.mean(values, axis=-1, keepdims=True)
    spread = jnp.mean(centre * centre, axis=-1, keepdims=True)
    scale = lax.rsqrt(spread + 1e-05)
    return centre * scale, scale


def bend(a):
    square = a * a
    t = jnp.tanh(HALF * a * (1.0 + 0.044715 * square))
    return t, 0.5 * (1.0 + t) + (0.5 * HALF) * a * (1.0 - t * t) * (1.0 + 0.134145 * square)


def norm_back(grad, scale, unit):
    return scale * (
        grad
        - jnp.mean(grad, axis=-1, keepdims=True)
        - unit * jnp.mean(grad * unit, axis=-1, keepdims=True)
    )


def over_rows(count, step):
    def run(i, carry):
        step(pl.ds(pl.multiple_of(i * CHUNK, CHUNK), CHUNK))
        return carry

    lax.fori_loop(0, count // CHUNK, run, 0, unroll=True)


def prepare_kernel(block, gain, hidden, weigh):
    def step(rows):
        unit, scale = normed(block[rows, :].astype(jnp.float32))
        a = unit * gain[...]
        t, slope = bend(a)
        hidden[rows, :] = (0.5 * a * (1.0 + t)).astype(jnp.bfloat16)
        weigh[rows, :] = slope * unit

    over_rows(block.shape[0], step)


def gather(where, pieces, whole, semaphores, slabs):
    copies = {}
    for k in slabs:
        for r in range(4):
            ref, slab = pieces[r][k]
            part = ref.shape[-2]
            place = pl.ds(pl.multiple_of(where[r], 128), part)
            copies[k, r] = pltpu.make_async_copy(
                ref.at[slab] if slab is not None else ref,
                whole.at[k, place],
                semaphores.at[k, r],
            )
            copies[k, r].start()

    def ready(k):
        for r in range(4):
            copies[k, r].wait()

    return ready


def pieces_of(weight, folded, weight_s, folded_s, up, down, up_s, down_s):
    return [
        [(weight, 0), (weight, 1), (weight, 2), (folded, None)],
        [(weight_s, 0), (weight_s, 1), (weight_s, 2), (folded_s, None)],
        [(up, 0), (up, 1), (down, 0), (down, 1)],
        [(up_s, 0), (up_s, 1), (down_s, 0), (down_s, 1)],
    ]


def middle_kernel(*refs):
    where, h0, h1, h2, e0, e1, e2, cotangent, gain = refs[:9]
    grad_mixed, sums, whole, mixed, grad2, partial, semaphores = refs[17:]
    ready = gather(where, pieces_of(*refs[9:17]), whole, semaphores, (3, 1, 0, 2))
    rows, width = mixed.shape
    channels = e0.shape[1]
    half = whole.shape[1] // 8

    ready(3)
    for j in range(2):
        held = jnp.concatenate(
            [whole[3, (2 * f + j) * half : (2 * f + j + 1) * half, :] for f in range(4)], axis=0
        )
        product = dot_t(cotangent[:, j * width : (j + 1) * width], held)
        grad2[...] = product if j == 0 else grad2[...] + product
    ready(1)
    mixed[...] = dot(h1[...], whole[1])
    ready(0)
    mixed[...] += dot(h0[...], whole[0])
    ready(2)
    mixed[...] += dot(h2[...], whole[2])
    partial[...] = jnp.zeros_like(partial)

    def step(at):
        unit, scale = normed(mixed[at, :].astype(jnp.bfloat16).astype(jnp.float32))
        unused, slope = bend(unit * gain[...])
        grad_a = grad2[at, :] * slope
        terms = grad_a * unit
        partial[...] += jnp.sum(terms.reshape(-1, 8, width), axis=0)
        grad_mixed[at, :] = norm_back(grad_a * gain[...], scale, unit).astype(jnp.bfloat16)

    over_rows(rows, step)

    def put(start, row):
        for i in range(0, row.shape[1], 128):
            j = (start + i) // 128
            sums[:, j : j + 1, :] = jnp.broadcast_to(
                row[:, i : i + 128][None], (sums.shape[0], 1, 128)
            )

    put(channels, jnp.sum(partial[...], axis=0, keepdims=True))
    for n in range(0, channels, 256):
        cols = slice(n, n + 256)
        terms = dot_t(grad_mixed[...], whole[0, cols, :]) * e0[:, cols]
        terms += dot_t(grad_mixed[...], whole[1, cols, :]) * e1[:, cols]
        terms += dot_t(grad_mixed[...], whole[2, cols, :]) * e2[:, cols]
        put(n, jnp.sum(terms, axis=0, keepdims=True))


def spread_kernel(arrived, sums):
    total = jnp.sum(arrived[...], axis=0, keepdims=True)
    sums[...] = jnp.broadcast_to(total, sums.shape)


def last_kernel(*refs):
    where, block, cotangent, ahead, here, behind, gain = refs[:7]
    result, whole, grads, semaphores = refs[15:]
    ready = gather(where, pieces_of(*refs[7:15]), whole, semaphores, (1, 0, 2))
    grads_of = ((1, here), (0, ahead), (2, behind))
    rows, channels = block.shape
    for k, grad in grads_of:
        ready(k)
        for n in range(0, channels, 256):
            cols = slice(n, n + 256)
            product = dot_t(grad[...], whole[k, cols, :])
            grads[:, cols] = product if k == 1 else grads[:, cols] + product

    def step(at):
        unit, scale = normed(block[at, :].astype(jnp.float32))
        unused, slope = bend(unit * gain[...])
        branch = norm_back(grads[at, :] * slope * gain[...], scale, unit)
        result[at, :] = (cotangent[at, :].astype(jnp.float32) + branch).astype(jnp.bfloat16)

    over_rows(rows, step)


VMEM_SPEC = pl.BlockSpec(memory_space=pltpu.VMEM)
SMEM_SPEC = pl.BlockSpec(memory_space=pltpu.SMEM)
ANY_SPEC = pl.BlockSpec(memory_space=pl.ANY)


def call(kernel, name, out_shape, scratch, flops, *operands, specs=None):
    moved = sum(v.size * v.dtype.itemsize for v in operands)
    return pl.pallas_call(
        kernel,
        name=name,
        out_shape=out_shape,
        in_specs=specs or [VMEM_SPEC] * len(operands),
        out_specs=jax.tree.map(lambda _: VMEM_SPEC, out_shape),
        scratch_shapes=scratch,
        cost_estimate=pl.CostEstimate(flops=flops, bytes_accessed=moved, transcendentals=0),
        compiler_params=pltpu.CompilerParams(vmem_limit_bytes=VMEM_LIMIT),
    )(*operands)


def dot(a, b):
    return lax.dot_general(a, b, (((1,), (0,)), ((), ())), preferred_element_type=jnp.float32)


def dot_t(a, b):
    return lax.dot_general(a, b, (((1,), (1,)), ((), ())), preferred_element_type=jnp.float32)


def body(block_input, weight, project, gain_first, gain_second, grad_output):
    samples, bins, channels = block_input.shape
    rows = samples * bins
    width = weight.shape[2]
    part = weight.shape[1]
    part_h = project.shape[0]
    inputs = block_input.reshape(rows, channels)
    cotangent = grad_output.reshape(rows, channels)

    own = lax.axis_index(FSDP)
    where = jnp.stack([(own ^ r) * part for r in range(4)])

    folded = jnp.concatenate([project[:, :width], project[:, width:]], axis=0)
    up = permute(weight[:2], along_y(1))
    down = permute(jnp.stack([weight[2], folded]), along_y(-1))
    weight_s, folded_s = permute(weight, sister), permute(folded, sister)
    up_s, down_s = permute(up, sister), permute(down, sister)
    pieces = (weight, folded, weight_s, folded_s, up, down, up_s, down_s)

    f32, bf16 = jnp.float32, jnp.bfloat16
    gain1, gain2 = gain_first[None], gain_second[None]

    def prepare(block):
        return call(
            prepare_kernel,
            "prepare",
            [jax.ShapeDtypeStruct(block.shape, bf16), jax.ShapeDtypeStruct(block.shape, f32)],
            [],
            40 * block.size,
            block,
            gain1,
        )

    own_pair = prepare(inputs)
    halo, own_pair = lax.optimization_barrier((inputs, own_pair))
    lagging = permute(halo, along_bins(1))
    leading = permute(halo, along_bins(-1))
    pairs = [prepare(lagging), own_pair, prepare(leading)]
    hiddens = [pair[0] for pair in pairs]
    weighs = [pair[1] for pair in pairs]

    work = 2 * rows * channels * width
    grad_mixed, sums = call(
        middle_kernel,
        "middle",
        [
            jax.ShapeDtypeStruct((rows, width), bf16),
            jax.ShapeDtypeStruct((32, (channels + width) // 128, 128), f32),
        ],
        [
            pltpu.VMEM((4, channels, width), bf16),
            pltpu.VMEM((rows, width), f32),
            pltpu.VMEM((rows, width), f32),
            pltpu.VMEM((8, width), f32),
            pltpu.SemaphoreType.DMA((4, 4)),
        ],
        8 * work,
        where,
        *hiddens,
        *weighs,
        cotangent,
        gain2,
        *pieces,
        specs=[SMEM_SPEC] + [VMEM_SPEC] * 8 + [ANY_SPEC] * 8,
    )
    ahead = permute(grad_mixed, along_bins(-1))
    behind = permute(grad_mixed, along_bins(1))

    sums = lax.all_to_all(sums, ("x", "yh", "yl", "c"), 0, 0)
    sums = call(
        spread_kernel, "spread", jax.ShapeDtypeStruct((16,) + sums.shape[1:], f32), [], 1, sums
    )
    ahead, behind, sums = lax.optimization_barrier((ahead, behind, sums))
    sums = jnp.sum(lax.all_to_all(sums, "z", 0, 0), axis=0).reshape(-1)

    grad_input = call(
        last_kernel,
        "last",
        jax.ShapeDtypeStruct(inputs.shape, bf16),
        [
            pltpu.VMEM((3, channels, width), bf16),
            pltpu.VMEM(inputs.shape, f32),
            pltpu.SemaphoreType.DMA((3, 4)),
        ],
        3 * work,
        where,
        inputs,
        cotangent,
        ahead,
        grad_mixed,
        behind,
        gain1,
        *pieces,
        specs=[SMEM_SPEC] + [VMEM_SPEC] * 6 + [ANY_SPEC] * 8,
    )
    return (grad_input.reshape(block_input.shape), sums[:channels], sums[channels:])


def solution(mesh):
    fine = Mesh(mesh.devices.reshape(SIZES), AXES)
    in_specs = (
        P(FSDP, SEQ, None),
        P(None, FSDP, None),
        P(FSDP, None),
        P(),
        P(),
        P(FSDP, SEQ, None),
    )
    out_specs = (P(FSDP, SEQ, None), P(), P())
    return jax.shard_map(body, mesh=fine, in_specs=in_specs, out_specs=out_specs, check_vma=False)
```

```python
import jax
import jax.numpy as jnp
import numpy as np
from jax import lax
from jax.experimental import pallas as pl
from jax.experimental.pallas import tpu as pltpu
from jax.sharding import Mesh
from jax.sharding import PartitionSpec as P

AXES = ("x", "yh", "z", "yl", "c")
SIZES = (4, 2, 16, 2, 2)
SEQ = ("x", "yh", "z")
FSDP = ("yl", "c")
HALF = 0.7978845608028654
VMEM_LIMIT = 16 * 1024 * 1024


def permute(value, target):
    pairs = []
    for place in np.ndindex(*SIZES):
        to = target(*place)
        if to is not None:
            pairs.append(
                (int(np.ravel_multi_index(place, SIZES)), int(np.ravel_multi_index(to, SIZES)))
            )
    return lax.ppermute(value, AXES, pairs)


def along_y(steps):
    def target(x, yh, z, yl, c):
        y = (2 * yh + yl + steps) % 4
        return (x, y // 2, z, y % 2, c)

    return target


def sister(x, yh, z, yl, c):
    return (x, yh, z, yl, 1 - c)


def antipode(x, yh, z, yl, c):
    return (x, 1 - yh, z, yl, c)


def hand_on(x, yh, z, yl, c):
    to = x + 1 - 2 * yh
    return (to, yh, z, yl, c) if 0 <= to < 4 else None


def second_neighbour(x, yh, z, yl, c):
    to = x + 1 - 2 * (1 - yh)
    return (to, 1 - yh, z, yl, c) if 0 <= to < 4 else None


CHUNK = 16


def normed(values):
    centre = values - jnp.mean(values, axis=-1, keepdims=True)
    spread = jnp.mean(centre * centre, axis=-1, keepdims=True)
    scale = lax.rsqrt(spread + 1e-05)
    return centre * scale, scale


def bend(a):
    square = a * a
    t = jnp.tanh(HALF * a * (1.0 + 0.044715 * square))
    return t, 0.5 * (1.0 + t) + (0.5 * HALF) * a * (1.0 - t * t) * (1.0 + 0.134145 * square)


def norm_back(grad, scale, unit):
    return scale * (
        grad
        - jnp.mean(grad, axis=-1, keepdims=True)
        - unit * jnp.mean(grad * unit, axis=-1, keepdims=True)
    )


def over_rows(count, step):
    def run(i, carry):
        step(pl.ds(pl.multiple_of(i * CHUNK, CHUNK), CHUNK))
        return carry

    lax.fori_loop(0, count // CHUNK, run, 0, unroll=True)


def prepare_kernel(block, gain, hidden, weigh):
    def step(rows):
        unit, scale = normed(block[rows, :].astype(jnp.float32))
        a = unit * gain[...]
        t, slope = bend(a)
        hidden[rows, :] = (0.5 * a * (1.0 + t)).astype(jnp.bfloat16)
        weigh[rows, :] = slope * unit

    over_rows(block.shape[0], step)


def gather(where, pieces, whole, semaphores, slabs):
    copies = {}
    for k in slabs:
        for r in range(4):
            ref, slab = pieces[r][k]
            part = ref.shape[-2]
            place = pl.ds(pl.multiple_of(where[r], 128), part)
            copies[k, r] = pltpu.make_async_copy(
                ref.at[slab] if slab is not None else ref,
                whole.at[k ^ where[4] if k in (0, 2) else k, place],
                semaphores.at[k, r],
            )
            copies[k, r].start()

    def ready(k):
        for r in range(4):
            copies[k, r].wait()

    return ready


def pieces_of(weight, folded, weight_s, folded_s, up, down, up_s, down_s):
    return [
        [(weight, 0), (weight, 1), (weight, 2), (folded, None)],
        [(weight_s, 0), (weight_s, 1), (weight_s, 2), (folded_s, None)],
        [(up, 0), (up, 1), (down, 0), (down, 1)],
        [(up_s, 0), (up_s, 1), (down_s, 0), (down_s, 1)],
    ]


def fetch(sources, places, semaphores):
    copies = [
        pltpu.make_async_copy(source, place, semaphores.at[i])
        for i, (source, place) in enumerate(zip(sources, places))
    ]
    for copy in copies:
        copy.start()
    return lambda i: copies[i].wait()


def early_kernel(*refs):
    where = refs[0]
    whole, mixed, grad2, semaphores, held_rows, row_semaphores = refs[11:]
    hidden, cotangent = held_rows.at[0], held_rows.at[1]
    fetched = fetch((refs[1], refs[2]), (hidden, cotangent), row_semaphores)
    ready = gather(where, pieces_of(*refs[3:11]), whole, semaphores, (3, 1, 0, 2))
    width = mixed.shape[1]
    half = whole.shape[1] // 8

    ready(3)
    fetched(1)
    for j in range(2):
        held = jnp.concatenate(
            [whole[3, (2 * f + j) * half : (2 * f + j + 1) * half, :] for f in range(4)], axis=0
        )
        product = dot_t(cotangent[:, j * width : (j + 1) * width], held)
        grad2[...] = product if j == 0 else grad2[...] + product
    ready(1)
    fetched(0)
    mixed[...] = dot(hidden[...], whole[1])
    ready(0)
    ready(2)


def middle_kernel(
    h0_away, h2, e0_away, e1_away, e2_away, whole, centre, grad2, gain, grad_mixed, sums, mixed,
    partial, h0, e0, e1, e2, semaphores,
):
    fetched = fetch((h0_away, e0_away, e1_away, e2_away), (h0, e0, e1, e2), semaphores)
    rows, width = mixed.shape
    channels = e0.shape[1]
    for n in range(0, width, 256):
        cols = slice(n, n + 256)
        mixed[:, cols] = centre[:, cols] + dot(h2[...], whole[2, :, cols])
    fetched(0)
    for n in range(0, width, 256):
        cols = slice(n, n + 256)
        mixed[:, cols] += dot(h0[...], whole[0, :, cols])
    partial[...] = jnp.zeros_like(partial)

    def step(at):
        unit, scale = normed(mixed[at, :].astype(jnp.bfloat16).astype(jnp.float32))
        unused, slope = bend(unit * gain[...])
        grad_a = grad2[at, :] * slope
        terms = grad_a * unit
        partial[...] += jnp.sum(terms.reshape(-1, 8, width), axis=0)
        grad_mixed[at, :] = norm_back(grad_a * gain[...], scale, unit).astype(jnp.bfloat16)

    over_rows(rows, step)

    def put(start, row):
        for i in range(0, row.shape[1], 128):
            j = (start + i) // 128
            sums[:, j : j + 1, :] = jnp.broadcast_to(
                row[:, i : i + 128][None], (sums.shape[0], 1, 128)
            )

    for i in range(1, 4):
        fetched(i)
    put(channels, jnp.sum(partial[...], axis=0, keepdims=True))
    for n in range(0, channels, 256):
        cols = slice(n, n + 256)
        terms = dot_t(grad_mixed[...], whole[0, cols, :]) * e0[:, cols]
        terms += dot_t(grad_mixed[...], whole[1, cols, :]) * e1[:, cols]
        terms += dot_t(grad_mixed[...], whole[2, cols, :]) * e2[:, cols]
        put(n, jnp.sum(terms, axis=0, keepdims=True))


def spread_kernel(arrived, sums):
    total = jnp.sum(arrived[...], axis=0, keepdims=True)
    sums[...] = jnp.broadcast_to(total, sums.shape)


def last_kernel(block, cotangent, near, here, far, whole, gain, result, grads):
    rows, channels = block.shape
    for n in range(0, channels, 256):
        cols = slice(n, n + 256)
        grads[:, cols] = (
            dot_t(here[...], whole[1, cols, :])
            + dot_t(near[...], whole[2, cols, :])
            + dot_t(far[...], whole[0, cols, :])
        )

    def step(at):
        unit, scale = normed(block[at, :].astype(jnp.float32))
        unused, slope = bend(unit * gain[...])
        branch = norm_back(grads[at, :] * slope * gain[...], scale, unit)
        result[at, :] = (cotangent[at, :].astype(jnp.float32) + branch).astype(jnp.bfloat16)

    over_rows(rows, step)


VMEM_SPEC = pl.BlockSpec(memory_space=pltpu.VMEM)
SMEM_SPEC = pl.BlockSpec(memory_space=pltpu.SMEM)
ANY_SPEC = pl.BlockSpec(memory_space=pl.ANY)


def call(kernel, name, out_shape, scratch, flops, *operands, specs=None):
    moved = sum(v.size * v.dtype.itemsize for v in operands)
    return pl.pallas_call(
        kernel,
        name=name,
        out_shape=out_shape,
        in_specs=specs or [VMEM_SPEC] * len(operands),
        out_specs=jax.tree.map(lambda _: VMEM_SPEC, out_shape),
        scratch_shapes=scratch,
        cost_estimate=pl.CostEstimate(flops=flops, bytes_accessed=moved, transcendentals=0),
        compiler_params=pltpu.CompilerParams(vmem_limit_bytes=VMEM_LIMIT),
    )(*operands)


def dot(a, b):
    return lax.dot_general(a, b, (((1,), (0,)), ((), ())), preferred_element_type=jnp.float32)


def dot_t(a, b):
    return lax.dot_general(a, b, (((1,), (1,)), ((), ())), preferred_element_type=jnp.float32)


def body(block_input, weight, project, gain_first, gain_second, grad_output):
    samples, bins, channels = block_input.shape
    rows = samples * bins
    width = weight.shape[2]
    part = weight.shape[1]
    part_h = project.shape[0]
    inputs = block_input.reshape(rows, channels)
    cotangent = grad_output.reshape(rows, channels)

    own = lax.axis_index(FSDP)
    where = jnp.stack([(own ^ r) * part for r in range(4)] + [2 - 2 * lax.axis_index("yh")])

    f32, bf16 = jnp.float32, jnp.bfloat16
    gain1, gain2 = gain_first[None], gain_second[None]

    def prepare(block):
        return call(
            prepare_kernel,
            "prepare",
            [jax.ShapeDtypeStruct(block.shape, bf16), jax.ShapeDtypeStruct(block.shape, f32)],
            [],
            40 * block.size,
            block,
            gain1,
        )

    near = permute(inputs, antipode)
    h1, e1 = prepare(inputs)
    folded = jnp.concatenate([project[:, :width], project[:, width:]], axis=0)
    sent_up, sent_down, sent, near = lax.optimization_barrier(
        (weight[:2], jnp.stack([weight[2], folded]), weight, near)
    )
    far = permute(near, hand_on)
    up, down = permute(sent_up, along_y(1)), permute(sent_down, along_y(-1))
    weight_s, folded_s = permute(sent, sister), permute(sent_down[1], sister)
    h0, e0 = prepare(near)
    up, down, far, h0, h1 = lax.optimization_barrier((up, down, far, h0, h1))
    up_s, down_s = permute(up, sister), permute(down, sister)
    pieces = (weight, folded, weight_s, folded_s, up, down, up_s, down_s)

    h2, e2 = prepare(far)

    work = 2 * rows * channels * width
    whole, centre, grad2 = call(
        early_kernel,
        "early",
        [
            jax.ShapeDtypeStruct((4, channels, width), bf16),
            jax.ShapeDtypeStruct((rows, width), f32),
            jax.ShapeDtypeStruct((rows, width), f32),
        ],
        [
            pltpu.SemaphoreType.DMA((4, 4)),
            pltpu.VMEM((2, rows, channels), bf16),
            pltpu.SemaphoreType.DMA((2,)),
        ],
        2 * work,
        where,
        h1,
        cotangent,
        *pieces,
        specs=[SMEM_SPEC] + [ANY_SPEC] * 10,
    )
    grad_mixed, sums = call(
        middle_kernel,
        "middle",
        [
            jax.ShapeDtypeStruct((rows, width), bf16),
            jax.ShapeDtypeStruct((32, (channels + width) // 128, 128), f32),
        ],
        [
            pltpu.VMEM((rows, width), f32),
            pltpu.VMEM((8, width), f32),
            pltpu.VMEM((rows, channels), bf16),
            pltpu.VMEM((rows, channels), f32),
            pltpu.VMEM((rows, channels), f32),
            pltpu.VMEM((rows, channels), f32),
            pltpu.SemaphoreType.DMA((4,)),
        ],
        5 * work,
        h0,
        h2,
        e0,
        e1,
        e2,
        whole,
        centre,
        grad2,
        gain2,
        specs=[ANY_SPEC, VMEM_SPEC] + [ANY_SPEC] * 3 + [VMEM_SPEC] * 4,
    )
    sums = lax.all_to_all(sums, ("x", "yh", "yl", "c"), 0, 0)
    sums = call(
        spread_kernel, "spread", jax.ShapeDtypeStruct((16,) + sums.shape[1:], f32), [], 1, sums
    )
    grad_mixed, sums = lax.optimization_barrier((grad_mixed, sums))
    near_grad = permute(grad_mixed, antipode)
    far_grad = permute(grad_mixed, second_neighbour)
    sums = lax.all_to_all(sums, "z", 0, 0)

    grad_input = call(
        last_kernel,
        "last",
        jax.ShapeDtypeStruct(inputs.shape, bf16),
        [pltpu.VMEM(inputs.shape, f32)],
        3 * work,
        inputs,
        cotangent,
        near_grad,
        grad_mixed,
        far_grad,
        whole,
        gain1,
    )
    lines = channels // 128
    first_sum = jnp.sum(sums[:, :lines], axis=0).reshape(-1)
    second_sum = jnp.sum(sums[:, lines:], axis=0).reshape(-1)
    return (grad_input.reshape(block_input.shape), first_sum, second_sum)


def solution(mesh):
    fine = Mesh(mesh.devices.reshape(SIZES), AXES)
    in_specs = (
        P(FSDP, SEQ, None),
        P(None, FSDP, None),
        P(FSDP, None),
        P(),
        P(),
        P(FSDP, SEQ, None),
    )
    out_specs = (P(FSDP, SEQ, None), P(), P())
    return jax.shard_map(body, mesh=fine, in_specs=in_specs, out_specs=out_specs, check_vma=False)
```

```python
import jax
import jax.numpy as jnp
import numpy as np
from jax import lax
from jax.experimental import pallas as pl
from jax.experimental.pallas import tpu as pltpu
from jax.sharding import Mesh
from jax.sharding import PartitionSpec as P

AXES = ("x", "yh", "z", "yl", "c")
SIZES = (4, 2, 16, 2, 2)
SEQ = ("x", "yh", "z")
FSDP = ("yl", "c")
HALF = 0.7978845608028654
VMEM_LIMIT = 16 * 1024 * 1024


def permute(value, target):
    pairs = []
    for place in np.ndindex(*SIZES):
        to = target(*place)
        if to is not None:
            pairs.append(
                (int(np.ravel_multi_index(place, SIZES)), int(np.ravel_multi_index(to, SIZES)))
            )
    return lax.ppermute(value, AXES, pairs)


def along_y(steps):
    def target(x, yh, z, yl, c):
        y = (2 * yh + yl + steps) % 4
        return (x, y // 2, z, y % 2, c)

    return target


def sister(x, yh, z, yl, c):
    return (x, yh, z, yl, 1 - c)


def antipode(x, yh, z, yl, c):
    return (x, 1 - yh, z, yl, c)


def hand_on(x, yh, z, yl, c):
    to = x + 1 - 2 * yh
    return (to, yh, z, yl, c) if 0 <= to < 4 else None


def second_neighbour(x, yh, z, yl, c):
    to = x + 1 - 2 * (1 - yh)
    return (to, 1 - yh, z, yl, c) if 0 <= to < 4 else None


CHUNK = 16


def normed(values):
    centre = values - jnp.mean(values, axis=-1, keepdims=True)
    spread = jnp.mean(centre * centre, axis=-1, keepdims=True)
    scale = lax.rsqrt(spread + 1e-05)
    return centre * scale, scale


def bend(a):
    square = a * a
    t = jnp.tanh(HALF * a * (1.0 + 0.044715 * square))
    return t, 0.5 * (1.0 + t) + (0.5 * HALF) * a * (1.0 - t * t) * (1.0 + 0.134145 * square)


def norm_back(grad, scale, unit):
    return scale * (
        grad
        - jnp.mean(grad, axis=-1, keepdims=True)
        - unit * jnp.mean(grad * unit, axis=-1, keepdims=True)
    )


def over_rows(count, step):
    def run(i, carry):
        step(pl.ds(pl.multiple_of(i * CHUNK, CHUNK), CHUNK))
        return carry

    lax.fori_loop(0, count // CHUNK, run, 0, unroll=True)


def prepare_kernel(block, gain, hidden, weigh):
    def step(rows):
        unit, scale = normed(block[rows, :].astype(jnp.float32))
        a = unit * gain[...]
        t, slope = bend(a)
        hidden[rows, :] = (0.5 * a * (1.0 + t)).astype(jnp.bfloat16)
        weigh[rows, :] = slope * unit

    over_rows(block.shape[0], step)


def gather(where, pieces, whole, semaphores, slabs, shards):
    copies = {}
    for k in slabs:
        for r in shards:
            ref, slab = pieces[r][k]
            part = ref.shape[-2]
            place = pl.ds(pl.multiple_of(where[r], 128), part)
            copies[k, r] = pltpu.make_async_copy(
                ref.at[slab] if slab is not None else ref,
                whole.at[k ^ where[4] if k in (0, 2) else k, place],
                semaphores.at[k, r],
            )
            copies[k, r].start()

    def ready(k):
        for r in shards:
            copies[k, r].wait()

    return ready


def place_kernel(where, weight, folded, weight_s, folded_s, up, down, whole, semaphores):
    pieces = [
        [(weight, 0), (weight, 1), (weight, 2), (folded, None)],
        [(weight_s, 0), (weight_s, 1), (weight_s, 2), (folded_s, None)],
        [(up, 0), (up, 1), (down, 0), (down, 1)],
    ]
    ready = gather(where, pieces, whole, semaphores, range(4), range(3))
    for k in range(4):
        ready(k)


def fetch(sources, places, semaphores):
    copies = [
        pltpu.make_async_copy(source, place, semaphores.at[i])
        for i, (source, place) in enumerate(zip(sources, places))
    ]
    for copy in copies:
        copy.start()
    return lambda i: copies[i].wait()


def early_kernel(
    where, hidden_away, cotangent_away, placed, up_s, down_s, whole, mixed, grad2, semaphores,
    held_rows, row_semaphores,
):
    hidden, cotangent = held_rows.at[0], held_rows.at[1]
    fetched = fetch((hidden_away, cotangent_away), (hidden, cotangent), row_semaphores)
    fourth = [(up_s, 0), (up_s, 1), (down_s, 0), (down_s, 1)]
    ready = gather(where, {3: fourth}, whole, semaphores, (3, 1, 0, 2), (3,))
    width = mixed.shape[1]
    half = whole.shape[1] // 8

    ready(3)
    fetched(1)
    for j in range(2):
        held = jnp.concatenate(
            [whole[3, (2 * f + j) * half : (2 * f + j + 1) * half, :] for f in range(4)], axis=0
        )
        product = dot_t(cotangent[:, j * width : (j + 1) * width], held)
        grad2[...] = product if j == 0 else grad2[...] + product
    ready(1)
    fetched(0)
    mixed[...] = dot(hidden[...], whole[1])
    ready(0)
    ready(2)


def middle_kernel(
    h0_away, h2, e0_away, e1_away, e2_away, whole, centre, grad2, gain, grad_mixed, sums, mixed,
    partial, h0, e0, e1, e2, semaphores,
):
    fetched = fetch((h0_away, e0_away, e1_away, e2_away), (h0, e0, e1, e2), semaphores)
    rows, width = mixed.shape
    channels = e0.shape[1]
    for n in range(0, width, 256):
        cols = slice(n, n + 256)
        mixed[:, cols] = centre[:, cols] + dot(h2[...], whole[2, :, cols])
    fetched(0)
    for n in range(0, width, 256):
        cols = slice(n, n + 256)
        mixed[:, cols] += dot(h0[...], whole[0, :, cols])
    partial[...] = jnp.zeros_like(partial)

    def step(at):
        unit, scale = normed(mixed[at, :].astype(jnp.bfloat16).astype(jnp.float32))
        unused, slope = bend(unit * gain[...])
        grad_a = grad2[at, :] * slope
        terms = grad_a * unit
        partial[...] += jnp.sum(terms.reshape(-1, 8, width), axis=0)
        grad_mixed[at, :] = norm_back(grad_a * gain[...], scale, unit).astype(jnp.bfloat16)

    over_rows(rows, step)

    def put(start, row):
        for i in range(0, row.shape[1], 128):
            j = (start + i) // 128
            sums[:, j : j + 1, :] = jnp.broadcast_to(
                row[:, i : i + 128][None], (sums.shape[0], 1, 128)
            )

    for i in range(1, 4):
        fetched(i)
    put(channels, jnp.sum(partial[...], axis=0, keepdims=True))
    for n in range(0, channels, 256):
        cols = slice(n, n + 256)
        terms = dot_t(grad_mixed[...], whole[0, cols, :]) * e0[:, cols]
        terms += dot_t(grad_mixed[...], whole[1, cols, :]) * e1[:, cols]
        terms += dot_t(grad_mixed[...], whole[2, cols, :]) * e2[:, cols]
        put(n, jnp.sum(terms, axis=0, keepdims=True))


def spread_kernel(arrived, sums):
    total = jnp.sum(arrived[...], axis=0, keepdims=True)
    sums[...] = jnp.broadcast_to(total, sums.shape)


def last_kernel(block, cotangent, near, here, far, whole, gain, result, grads):
    rows, channels = block.shape
    for n in range(0, channels, 256):
        cols = slice(n, n + 256)
        grads[:, cols] = (
            dot_t(here[...], whole[1, cols, :])
            + dot_t(near[...], whole[2, cols, :])
            + dot_t(far[...], whole[0, cols, :])
        )

    def step(at):
        unit, scale = normed(block[at, :].astype(jnp.float32))
        unused, slope = bend(unit * gain[...])
        branch = norm_back(grads[at, :] * slope * gain[...], scale, unit)
        result[at, :] = (cotangent[at, :].astype(jnp.float32) + branch).astype(jnp.bfloat16)

    over_rows(rows, step)


VMEM_SPEC = pl.BlockSpec(memory_space=pltpu.VMEM)
SMEM_SPEC = pl.BlockSpec(memory_space=pltpu.SMEM)
ANY_SPEC = pl.BlockSpec(memory_space=pl.ANY)


def call(kernel, name, out_shape, scratch, flops, *operands, specs=None, aliases=None):
    moved = sum(v.size * v.dtype.itemsize for v in operands)
    return pl.pallas_call(
        kernel,
        name=name,
        out_shape=out_shape,
        in_specs=specs or [VMEM_SPEC] * len(operands),
        out_specs=jax.tree.map(lambda _: VMEM_SPEC, out_shape),
        scratch_shapes=scratch,
        input_output_aliases=aliases or {},
        cost_estimate=pl.CostEstimate(flops=flops, bytes_accessed=moved, transcendentals=0),
        compiler_params=pltpu.CompilerParams(vmem_limit_bytes=VMEM_LIMIT),
    )(*operands)


def dot(a, b):
    return lax.dot_general(a, b, (((1,), (0,)), ((), ())), preferred_element_type=jnp.float32)


def dot_t(a, b):
    return lax.dot_general(a, b, (((1,), (1,)), ((), ())), preferred_element_type=jnp.float32)


def body(block_input, weight, project, gain_first, gain_second, grad_output):
    samples, bins, channels = block_input.shape
    rows = samples * bins
    width = weight.shape[2]
    part = weight.shape[1]
    part_h = project.shape[0]
    inputs = block_input.reshape(rows, channels)
    cotangent = grad_output.reshape(rows, channels)

    own = lax.axis_index(FSDP)
    where = jnp.stack([(own ^ r) * part for r in range(4)] + [2 - 2 * lax.axis_index("yh")])

    f32, bf16 = jnp.float32, jnp.bfloat16
    gain1, gain2 = gain_first[None], gain_second[None]

    def prepare(block):
        return call(
            prepare_kernel,
            "prepare",
            [jax.ShapeDtypeStruct(block.shape, bf16), jax.ShapeDtypeStruct(block.shape, f32)],
            [],
            40 * block.size,
            block,
            gain1,
        )

    near = permute(inputs, antipode)
    h1, e1 = prepare(inputs)
    folded = jnp.concatenate([project[:, :width], project[:, width:]], axis=0)
    sent_up, sent_down, sent, near = lax.optimization_barrier(
        (weight[:2], jnp.stack([weight[2], folded]), weight, near)
    )
    far = permute(near, hand_on)
    up, down = permute(sent_up, along_y(1)), permute(sent_down, along_y(-1))
    weight_s, folded_s = permute(sent, sister), permute(sent_down[1], sister)
    h0, e0 = prepare(near)
    h2, e2 = prepare(far)
    up, down, h0, h1, h2, folded_s = lax.optimization_barrier((up, down, h0, h1, h2, folded_s))
    up_s, down_s = permute(up, sister), permute(down, sister)
    pieces = (weight, folded, weight_s, folded_s, up, down, up_s, down_s)


    work = 2 * rows * channels * width
    kernels_whole = jax.ShapeDtypeStruct((4, channels, width), bf16)
    placed = call(
        place_kernel,
        "place",
        kernels_whole,
        [pltpu.SemaphoreType.DMA((4, 4))],
        work,
        where,
        *pieces[:6],
        specs=[SMEM_SPEC] + [ANY_SPEC] * 6,
    )
    whole, centre, grad2 = call(
        early_kernel,
        "early",
        [
            kernels_whole,
            jax.ShapeDtypeStruct((rows, width), f32),
            jax.ShapeDtypeStruct((rows, width), f32),
        ],
        [
            pltpu.SemaphoreType.DMA((4, 4)),
            pltpu.VMEM((2, rows, channels), bf16),
            pltpu.SemaphoreType.DMA((2,)),
        ],
        2 * work,
        where,
        h1,
        cotangent,
        placed,
        *pieces[6:],
        specs=[SMEM_SPEC] + [ANY_SPEC] * 2 + [VMEM_SPEC] + [ANY_SPEC] * 2,
        aliases={3: 0},
    )
    grad_mixed, sums = call(
        middle_kernel,
        "middle",
        [
            jax.ShapeDtypeStruct((rows, width), bf16),
            jax.ShapeDtypeStruct((32, (channels + width) // 128, 128), f32),
        ],
        [
            pltpu.VMEM((rows, width), f32),
            pltpu.VMEM((8, width), f32),
            pltpu.VMEM((rows, channels), bf16),
            pltpu.VMEM((rows, channels), f32),
            pltpu.VMEM((rows, channels), f32),
            pltpu.VMEM((rows, channels), f32),
            pltpu.SemaphoreType.DMA((4,)),
        ],
        5 * work,
        h0,
        h2,
        e0,
        e1,
        e2,
        whole,
        centre,
        grad2,
        gain2,
        specs=[ANY_SPEC, VMEM_SPEC] + [ANY_SPEC] * 3 + [VMEM_SPEC] * 4,
    )
    sums = lax.all_to_all(sums, ("x", "yh", "yl", "c"), 0, 0)
    sums = call(
        spread_kernel, "spread", jax.ShapeDtypeStruct((16,) + sums.shape[1:], f32), [], 1, sums
    )
    grad_mixed, sums = lax.optimization_barrier((grad_mixed, sums))
    near_grad = permute(grad_mixed, antipode)
    far_grad = permute(grad_mixed, second_neighbour)
    sums = lax.all_to_all(sums, "z", 0, 0)

    grad_input = call(
        last_kernel,
        "last",
        jax.ShapeDtypeStruct(inputs.shape, bf16),
        [pltpu.VMEM(inputs.shape, f32)],
        3 * work,
        inputs,
        cotangent,
        near_grad,
        grad_mixed,
        far_grad,
        whole,
        gain1,
    )
    lines = channels // 128
    first_sum = jnp.sum(sums[:, :lines], axis=0).reshape(-1)
    second_sum = jnp.sum(sums[:, lines:], axis=0).reshape(-1)
    return (grad_input.reshape(block_input.shape), first_sum, second_sum)


def solution(mesh):
    fine = Mesh(mesh.devices.reshape(SIZES), AXES)
    in_specs = (
        P(FSDP, SEQ, None),
        P(None, FSDP, None),
        P(FSDP, None),
        P(),
        P(),
        P(FSDP, SEQ, None),
    )
    out_specs = (P(FSDP, SEQ, None), P(), P())
    return jax.shard_map(body, mesh=fine, in_specs=in_specs, out_specs=out_specs, check_vma=False)
```

```python
import jax
import jax.numpy as jnp
import numpy as np
from jax import lax
from jax.experimental import pallas as pl
from jax.experimental.pallas import tpu as pltpu
from jax.sharding import Mesh
from jax.sharding import PartitionSpec as P

AXES = ("x", "yh", "z", "yl", "c")
SIZES = (4, 2, 16, 2, 2)
SEQ = ("x", "yh", "z")
FSDP = ("yl", "c")
HALF = 0.7978845608028654
VMEM_LIMIT = 16 * 1024 * 1024


def permute(value, target):
    pairs = []
    for place in np.ndindex(*SIZES):
        to = target(*place)
        if to is not None:
            pairs.append(
                (int(np.ravel_multi_index(place, SIZES)), int(np.ravel_multi_index(to, SIZES)))
            )
    return lax.ppermute(value, AXES, pairs)


def along_y(steps):
    def target(x, yh, z, yl, c):
        y = (2 * yh + yl + steps) % 4
        return (x, y // 2, z, y % 2, c)

    return target


def sister(x, yh, z, yl, c):
    return (x, yh, z, yl, 1 - c)


def antipode(x, yh, z, yl, c):
    return (x, 1 - yh, z, yl, c)


def hand_on(x, yh, z, yl, c):
    to = x + 1 - 2 * yh
    return (to, yh, z, yl, c) if 0 <= to < 4 else None


def second_neighbour(x, yh, z, yl, c):
    to = x + 1 - 2 * (1 - yh)
    return (to, 1 - yh, z, yl, c) if 0 <= to < 4 else None


CHUNK = 16


def normed(values):
    centre = values - jnp.mean(values, axis=-1, keepdims=True)
    spread = jnp.mean(centre * centre, axis=-1, keepdims=True)
    scale = lax.rsqrt(spread + 1e-05)
    return centre * scale, scale


def bend(a):
    square = a * a
    t = jnp.tanh(HALF * a * (1.0 + 0.044715 * square))
    return t, 0.5 * (1.0 + t) + (0.5 * HALF) * a * (1.0 - t * t) * (1.0 + 0.134145 * square)


def norm_back(grad, scale, unit):
    return scale * (
        grad
        - jnp.mean(grad, axis=-1, keepdims=True)
        - unit * jnp.mean(grad * unit, axis=-1, keepdims=True)
    )


def over_rows(count, step):
    def run(i, carry):
        step(pl.ds(pl.multiple_of(i * CHUNK, CHUNK), CHUNK))
        return carry

    lax.fori_loop(0, count // CHUNK, run, 0, unroll=True)


def prepare_kernel(block, gain, hidden, weigh):
    def step(rows):
        unit, scale = normed(block[rows, :].astype(jnp.float32))
        a = unit * gain[...]
        t, slope = bend(a)
        hidden[rows, :] = (0.5 * a * (1.0 + t)).astype(jnp.bfloat16)
        weigh[rows, :] = slope * unit

    over_rows(block.shape[0], step)


def gather(where, pieces, whole, semaphores, slabs, shards):
    copies = {}
    for k in slabs:
        for r in shards:
            ref, slab = pieces[r][k]
            part = ref.shape[-2]
            place = pl.ds(pl.multiple_of(where[r], 128), part)
            copies[k, r] = pltpu.make_async_copy(
                ref.at[slab] if slab is not None else ref,
                whole.at[k ^ where[4] if k in (0, 2) else k, place],
                semaphores.at[k, r],
            )
            copies[k, r].start()

    def ready(k):
        for r in shards:
            copies[k, r].wait()

    return ready


def place_kernel(where, weight, folded, weight_s, folded_s, up, down, whole, semaphores):
    pieces = [
        [(weight, 0), (weight, 1), (weight, 2), (folded, None)],
        [(weight_s, 0), (weight_s, 1), (weight_s, 2), (folded_s, None)],
        [(up, 0), (up, 1), (down, 0), (down, 1)],
    ]
    ready = gather(where, pieces, whole, semaphores, range(4), range(3))
    for k in range(4):
        ready(k)


def fetch(sources, places, semaphores):
    copies = [
        pltpu.make_async_copy(source, place, semaphores.at[i])
        for i, (source, place) in enumerate(zip(sources, places))
    ]
    for copy in copies:
        copy.start()
    return lambda i: copies[i].wait()


def early_kernel(
    where, hidden_away, cotangent_away, placed, up_s, down_s, whole, mixed, grad2, semaphores,
    held_rows, row_semaphores,
):
    hidden, cotangent = held_rows.at[0], held_rows.at[1]
    fetched = fetch((hidden_away, cotangent_away), (hidden, cotangent), row_semaphores)
    fourth = [(up_s, 0), (up_s, 1), (down_s, 0), (down_s, 1)]
    ready = gather(where, {3: fourth}, whole, semaphores, (3, 1, 0, 2), (3,))
    width = mixed.shape[1]
    half = whole.shape[1] // 8

    ready(3)
    fetched(1)
    for j in range(2):
        held = jnp.concatenate(
            [whole[3, (2 * f + j) * half : (2 * f + j + 1) * half, :] for f in range(4)], axis=0
        )
        product = dot_t(cotangent[:, j * width : (j + 1) * width], held)
        grad2[...] = product if j == 0 else grad2[...] + product
    ready(1)
    fetched(0)
    mixed[...] = dot(hidden[...], whole[1])
    ready(0)
    ready(2)


def middle_kernel(
    h0_away, h2, e0_away, e1_away, e2_away, whole, centre, grad2, gain, grad_mixed, sums, mixed,
    partial, h0, e0, e1, e2, semaphores,
):
    fetched = fetch((h0_away, e0_away, e1_away, e2_away), (h0, e0, e1, e2), semaphores)
    rows, width = mixed.shape
    channels = e0.shape[1]
    for n in range(0, width, 256):
        cols = slice(n, n + 256)
        mixed[:, cols] = centre[:, cols] + dot(h2[...], whole[2, :, cols])
    fetched(0)
    for n in range(0, width, 256):
        cols = slice(n, n + 256)
        mixed[:, cols] += dot(h0[...], whole[0, :, cols])
    partial[...] = jnp.zeros_like(partial)

    def step(at):
        unit, scale = normed(mixed[at, :].astype(jnp.bfloat16).astype(jnp.float32))
        unused, slope = bend(unit * gain[...])
        grad_a = grad2[at, :] * slope
        terms = grad_a * unit
        partial[...] += jnp.sum(terms.reshape(-1, 8, width), axis=0)
        grad_mixed[at, :] = norm_back(grad_a * gain[...], scale, unit).astype(jnp.bfloat16)

    over_rows(rows, step)

    def put(start, row):
        for i in range(0, row.shape[1], 128):
            j = (start + i) // 128
            sums[:, j : j + 1, :] = jnp.broadcast_to(
                row[:, i : i + 128][None], (sums.shape[0], 1, 128)
            )

    for i in range(1, 4):
        fetched(i)
    put(channels, jnp.sum(partial[...], axis=0, keepdims=True))
    for n in range(0, channels, 256):
        cols = slice(n, n + 256)
        terms = dot_t(grad_mixed[...], whole[0, cols, :]) * e0[:, cols]
        terms += dot_t(grad_mixed[...], whole[1, cols, :]) * e1[:, cols]
        terms += dot_t(grad_mixed[...], whole[2, cols, :]) * e2[:, cols]
        put(n, jnp.sum(terms, axis=0, keepdims=True))


def spread_kernel(arrived, sums):
    total = jnp.sum(arrived[...], axis=0, keepdims=True)
    sums[...] = jnp.broadcast_to(total, sums.shape)


def last_kernel(block, cotangent, near, here, far, whole, gain, result, grads):
    rows, channels = block.shape
    for n in range(0, channels, 256):
        cols = slice(n, n + 256)
        grads[:, cols] = (
            dot_t(here[...], whole[1, cols, :])
            + dot_t(near[...], whole[2, cols, :])
            + dot_t(far[...], whole[0, cols, :])
        )

    def step(at):
        unit, scale = normed(block[at, :].astype(jnp.float32))
        unused, slope = bend(unit * gain[...])
        branch = norm_back(grads[at, :] * slope * gain[...], scale, unit)
        result[at, :] = (cotangent[at, :].astype(jnp.float32) + branch).astype(jnp.bfloat16)

    over_rows(rows, step)


VMEM_SPEC = pl.BlockSpec(memory_space=pltpu.VMEM)
SMEM_SPEC = pl.BlockSpec(memory_space=pltpu.SMEM)
ANY_SPEC = pl.BlockSpec(memory_space=pl.ANY)


def call(kernel, name, out_shape, scratch, flops, *operands, specs=None, aliases=None):
    moved = sum(v.size * v.dtype.itemsize for v in operands)
    return pl.pallas_call(
        kernel,
        name=name,
        out_shape=out_shape,
        in_specs=specs or [VMEM_SPEC] * len(operands),
        out_specs=jax.tree.map(lambda _: VMEM_SPEC, out_shape),
        scratch_shapes=scratch,
        input_output_aliases=aliases or {},
        cost_estimate=pl.CostEstimate(flops=flops, bytes_accessed=moved, transcendentals=0),
        compiler_params=pltpu.CompilerParams(vmem_limit_bytes=VMEM_LIMIT),
    )(*operands)


def dot(a, b):
    return lax.dot_general(a, b, (((1,), (0,)), ((), ())), preferred_element_type=jnp.float32)


def dot_t(a, b):
    return lax.dot_general(a, b, (((1,), (1,)), ((), ())), preferred_element_type=jnp.float32)


def body(block_input, weight, project, gain_first, gain_second, grad_output):
    samples, bins, channels = block_input.shape
    rows = samples * bins
    width = weight.shape[2]
    part = weight.shape[1]
    part_h = project.shape[0]
    inputs = block_input.reshape(rows, channels)
    cotangent = grad_output.reshape(rows, channels)

    own = lax.axis_index(FSDP)
    where = jnp.stack([(own ^ r) * part for r in range(4)] + [2 - 2 * lax.axis_index("yh")])

    f32, bf16 = jnp.float32, jnp.bfloat16
    gain1, gain2 = gain_first[None], gain_second[None]

    def prepare(block):
        return call(
            prepare_kernel,
            "prepare",
            [jax.ShapeDtypeStruct(block.shape, bf16), jax.ShapeDtypeStruct(block.shape, f32)],
            [],
            40 * block.size,
            block,
            gain1,
        )

    near = permute(inputs, antipode)
    h1, e1 = prepare(inputs)
    folded = jnp.concatenate([project[:, :width], project[:, width:]], axis=0)
    sent_up, sent_down, sent, near = lax.optimization_barrier(
        (weight[:2], jnp.stack([weight[2], folded]), weight, near)
    )
    far = permute(near, hand_on)
    up, down = permute(sent_up, along_y(1)), permute(sent_down, along_y(-1))
    weight_s, folded_s = permute(sent, sister), permute(sent_down[1], sister)
    h0, e0 = prepare(near)
    h2, e2 = prepare(far)
    up, down, h0, h1, h2, folded_s = lax.optimization_barrier((up, down, h0, h1, h2, folded_s))
    up_s, down_s = permute(up, sister), permute(down, sister)
    pieces = (weight, folded, weight_s, folded_s, up, down, up_s, down_s)


    work = 2 * rows * channels * width
    kernels_whole = jax.ShapeDtypeStruct((4, channels, width), bf16)
    placed = call(
        place_kernel,
        "place",
        kernels_whole,
        [pltpu.SemaphoreType.DMA((4, 4))],
        work,
        where,
        *pieces[:6],
        specs=[SMEM_SPEC] + [ANY_SPEC] * 6,
    )
    whole, centre, grad2 = call(
        early_kernel,
        "early",
        [
            kernels_whole,
            jax.ShapeDtypeStruct((rows, width), f32),
            jax.ShapeDtypeStruct((rows, width), f32),
        ],
        [
            pltpu.SemaphoreType.DMA((4, 4)),
            pltpu.VMEM((2, rows, channels), bf16),
            pltpu.SemaphoreType.DMA((2,)),
        ],
        2 * work,
        where,
        h1,
        cotangent,
        placed,
        *pieces[6:],
        specs=[SMEM_SPEC] + [ANY_SPEC] * 2 + [VMEM_SPEC] + [ANY_SPEC] * 2,
        aliases={3: 0},
    )
    grad_mixed, sums = call(
        middle_kernel,
        "middle",
        [
            jax.ShapeDtypeStruct((rows, width), bf16),
            jax.ShapeDtypeStruct((16, (channels + width) // 128, 128), f32),
        ],
        [
            pltpu.VMEM((rows, width), f32),
            pltpu.VMEM((8, width), f32),
            pltpu.VMEM((rows, channels), bf16),
            pltpu.VMEM((rows, channels), f32),
            pltpu.VMEM((rows, channels), f32),
            pltpu.VMEM((rows, channels), f32),
            pltpu.SemaphoreType.DMA((4,)),
        ],
        5 * work,
        h0,
        h2,
        e0,
        e1,
        e2,
        whole,
        centre,
        grad2,
        gain2,
        specs=[ANY_SPEC, VMEM_SPEC] + [ANY_SPEC] * 3 + [VMEM_SPEC] * 4,
    )
    near_grad = permute(grad_mixed, antipode)
    far_grad = permute(grad_mixed, second_neighbour)
    sums = lax.all_to_all(sums, "z", 0, 0)
    sums = call(
        spread_kernel, "spread", jax.ShapeDtypeStruct((32,) + sums.shape[1:], f32), [], 1, sums
    )
    sums = lax.all_to_all(sums, ("x", "yh", "yl", "c"), 0, 0)

    grad_input = call(
        last_kernel,
        "last",
        jax.ShapeDtypeStruct(inputs.shape, bf16),
        [pltpu.VMEM(inputs.shape, f32)],
        3 * work,
        inputs,
        cotangent,
        near_grad,
        grad_mixed,
        far_grad,
        whole,
        gain1,
    )
    lines = channels // 128
    first_sum = jnp.sum(sums[:, :lines], axis=0).reshape(-1)
    second_sum = jnp.sum(sums[:, lines:], axis=0).reshape(-1)
    return (grad_input.reshape(block_input.shape), first_sum, second_sum)


def solution(mesh):
    fine = Mesh(mesh.devices.reshape(SIZES), AXES)
    in_specs = (
        P(FSDP, SEQ, None),
        P(None, FSDP, None),
        P(FSDP, None),
        P(),
        P(),
        P(FSDP, SEQ, None),
    )
    out_specs = (P(FSDP, SEQ, None), P(), P())
    return jax.shard_map(body, mesh=fine, in_specs=in_specs, out_specs=out_specs, check_vma=False)
```

```python
import jax
import jax.numpy as jnp
import numpy as np
from jax import lax
from jax.experimental import pallas as pl
from jax.experimental.pallas import tpu as pltpu
from jax.sharding import Mesh
from jax.sharding import PartitionSpec as P

AXES = ("x", "yh", "z", "yl", "c")
SIZES = (4, 2, 16, 2, 2)
SEQ = ("x", "yh", "z")
FSDP = ("yl", "c")
HALF = 0.7978845608028654
VMEM_LIMIT = 16 * 1024 * 1024


def permute(value, target):
    pairs = []
    for place in np.ndindex(*SIZES):
        to = target(*place)
        if to is not None:
            pairs.append(
                (int(np.ravel_multi_index(place, SIZES)), int(np.ravel_multi_index(to, SIZES)))
            )
    return lax.ppermute(value, AXES, pairs)


def along_y(steps):
    def target(x, yh, z, yl, c):
        y = (2 * yh + yl + steps) % 4
        return (x, y // 2, z, y % 2, c)

    return target


def sister(x, yh, z, yl, c):
    return (x, yh, z, yl, 1 - c)


def antipode(x, yh, z, yl, c):
    return (x, 1 - yh, z, yl, c)


def hand_on(x, yh, z, yl, c):
    to = x + 1 - 2 * yh
    return (to, yh, z, yl, c) if 0 <= to < 4 else None


def second_neighbour(x, yh, z, yl, c):
    to = x + 1 - 2 * (1 - yh)
    return (to, 1 - yh, z, yl, c) if 0 <= to < 4 else None


CHUNK = 16


def normed(values):
    centre = values - jnp.mean(values, axis=-1, keepdims=True)
    spread = jnp.mean(centre * centre, axis=-1, keepdims=True)
    scale = lax.rsqrt(spread + 1e-05)
    return centre * scale, scale


def bend(a):
    square = a * a
    t = jnp.tanh(HALF * a * (1.0 + 0.044715 * square))
    return t, 0.5 * (1.0 + t) + (0.5 * HALF) * a * (1.0 - t * t) * (1.0 + 0.134145 * square)


def norm_back(grad, scale, unit):
    return scale * (
        grad
        - jnp.mean(grad, axis=-1, keepdims=True)
        - unit * jnp.mean(grad * unit, axis=-1, keepdims=True)
    )


def over_rows(count, step):
    def run(i, carry):
        step(pl.ds(pl.multiple_of(i * CHUNK, CHUNK), CHUNK))
        return carry

    lax.fori_loop(0, count // CHUNK, run, 0, unroll=True)


def prepare_kernel(block, gain, hidden, weigh):
    def step(rows):
        unit, scale = normed(block[rows, :].astype(jnp.float32))
        a = unit * gain[...]
        t, slope = bend(a)
        hidden[rows, :] = (0.5 * a * (1.0 + t)).astype(jnp.bfloat16)
        weigh[rows, :] = (slope * unit).astype(jnp.bfloat16)

    over_rows(block.shape[0], step)


def gather(where, pieces, whole, semaphores, slabs, shards):
    copies = {}
    for k in slabs:
        for r in shards:
            ref, slab = pieces[r][k]
            part = ref.shape[-2]
            place = pl.ds(pl.multiple_of(where[r], 128), part)
            copies[k, r] = pltpu.make_async_copy(
                ref.at[slab] if slab is not None else ref,
                whole.at[k ^ where[4] if k in (0, 2) else k, place],
                semaphores.at[k, r],
            )
            copies[k, r].start()

    def ready(k):
        for r in shards:
            copies[k, r].wait()

    return ready


def place_kernel(where, weight, folded, weight_s, folded_s, up, down, whole, semaphores):
    pieces = [
        [(weight, 0), (weight, 1), (weight, 2), (folded, None)],
        [(weight_s, 0), (weight_s, 1), (weight_s, 2), (folded_s, None)],
        [(up, 0), (up, 1), (down, 0), (down, 1)],
    ]
    ready = gather(where, pieces, whole, semaphores, range(4), range(3))
    for k in range(4):
        ready(k)


def fetch(sources, places, semaphores):
    copies = [
        pltpu.make_async_copy(source, place, semaphores.at[i])
        for i, (source, place) in enumerate(zip(sources, places))
    ]
    for copy in copies:
        copy.start()
    return lambda i: copies[i].wait()


def early_kernel(
    where, hidden_away, cotangent_away, placed, up_s, down_s, whole, mixed, grad2, semaphores,
    held_rows, row_semaphores,
):
    hidden, cotangent = held_rows.at[0], held_rows.at[1]
    fetched = fetch((hidden_away, cotangent_away), (hidden, cotangent), row_semaphores)
    fourth = [(up_s, 0), (up_s, 1), (down_s, 0), (down_s, 1)]
    ready = gather(where, {3: fourth}, whole, semaphores, (3, 1, 0, 2), (3,))
    width = mixed.shape[1]
    half = whole.shape[1] // 8

    ready(3)
    fetched(1)
    for j in range(2):
        held = jnp.concatenate(
            [whole[3, (2 * f + j) * half : (2 * f + j + 1) * half, :] for f in range(4)], axis=0
        )
        product = dot_t(cotangent[:, j * width : (j + 1) * width], held)
        grad2[...] = product if j == 0 else grad2[...] + product
    ready(1)
    fetched(0)
    mixed[...] = dot(hidden[...], whole[1])
    ready(0)
    ready(2)


def middle_kernel(
    h0_away, h2, e0_away, e1_away, e2_away, whole, centre, grad2, gain, grad_mixed, sums, mixed,
    partial, h0, e0, e1, e2, semaphores,
):
    fetched = fetch((h0_away, e0_away, e1_away, e2_away), (h0, e0, e1, e2), semaphores)
    rows, width = mixed.shape
    channels = e0.shape[1]
    for n in range(0, width, 256):
        cols = slice(n, n + 256)
        mixed[:, cols] = centre[:, cols] + dot(h2[...], whole[2, :, cols])
    fetched(0)
    for n in range(0, width, 256):
        cols = slice(n, n + 256)
        mixed[:, cols] += dot(h0[...], whole[0, :, cols])
    partial[...] = jnp.zeros_like(partial)

    def step(at):
        unit, scale = normed(mixed[at, :].astype(jnp.bfloat16).astype(jnp.float32))
        unused, slope = bend(unit * gain[...])
        grad_a = grad2[at, :] * slope
        terms = grad_a * unit
        partial[...] += jnp.sum(terms.reshape(-1, 8, width), axis=0)
        grad_mixed[at, :] = norm_back(grad_a * gain[...], scale, unit).astype(jnp.bfloat16)

    over_rows(rows, step)

    def put(start, row):
        for i in range(0, row.shape[1], 128):
            j = (start + i) // 128
            sums[:, j : j + 1, :] = jnp.broadcast_to(
                row[:, i : i + 128][None], (sums.shape[0], 1, 128)
            )

    for i in range(1, 4):
        fetched(i)
    put(channels, jnp.sum(partial[...], axis=0, keepdims=True))
    for n in range(0, channels, 256):
        cols = slice(n, n + 256)
        terms = dot_t(grad_mixed[...], whole[0, cols, :]) * e0[:, cols].astype(jnp.float32)
        terms += dot_t(grad_mixed[...], whole[1, cols, :]) * e1[:, cols].astype(jnp.float32)
        terms += dot_t(grad_mixed[...], whole[2, cols, :]) * e2[:, cols].astype(jnp.float32)
        put(n, jnp.sum(terms, axis=0, keepdims=True))


def spread_kernel(arrived, sums):
    total = jnp.sum(arrived[...], axis=0, keepdims=True)
    sums[...] = jnp.broadcast_to(total, sums.shape)


def last_kernel(block, cotangent, near, here, far, whole, gain, result, grads):
    rows, channels = block.shape
    for n in range(0, channels, 256):
        cols = slice(n, n + 256)
        grads[:, cols] = (
            dot_t(here[...], whole[1, cols, :])
            + dot_t(near[...], whole[2, cols, :])
            + dot_t(far[...], whole[0, cols, :])
        )

    def step(at):
        unit, scale = normed(block[at, :].astype(jnp.float32))
        unused, slope = bend(unit * gain[...])
        branch = norm_back(grads[at, :] * slope * gain[...], scale, unit)
        result[at, :] = (cotangent[at, :].astype(jnp.float32) + branch).astype(jnp.bfloat16)

    over_rows(rows, step)


VMEM_SPEC = pl.BlockSpec(memory_space=pltpu.VMEM)
SMEM_SPEC = pl.BlockSpec(memory_space=pltpu.SMEM)
ANY_SPEC = pl.BlockSpec(memory_space=pl.ANY)


def call(kernel, name, out_shape, scratch, flops, *operands, specs=None, aliases=None):
    moved = sum(v.size * v.dtype.itemsize for v in operands)
    return pl.pallas_call(
        kernel,
        name=name,
        out_shape=out_shape,
        in_specs=specs or [VMEM_SPEC] * len(operands),
        out_specs=jax.tree.map(lambda _: VMEM_SPEC, out_shape),
        scratch_shapes=scratch,
        input_output_aliases=aliases or {},
        cost_estimate=pl.CostEstimate(flops=flops, bytes_accessed=moved, transcendentals=0),
        compiler_params=pltpu.CompilerParams(vmem_limit_bytes=VMEM_LIMIT),
    )(*operands)


def dot(a, b):
    return lax.dot_general(a, b, (((1,), (0,)), ((), ())), preferred_element_type=jnp.float32)


def dot_t(a, b):
    return lax.dot_general(a, b, (((1,), (1,)), ((), ())), preferred_element_type=jnp.float32)


def body(block_input, weight, project, gain_first, gain_second, grad_output):
    samples, bins, channels = block_input.shape
    rows = samples * bins
    width = weight.shape[2]
    part = weight.shape[1]
    part_h = project.shape[0]
    inputs = block_input.reshape(rows, channels)
    cotangent = grad_output.reshape(rows, channels)

    own = lax.axis_index(FSDP)
    where = jnp.stack([(own ^ r) * part for r in range(4)] + [2 - 2 * lax.axis_index("yh")])

    f32, bf16 = jnp.float32, jnp.bfloat16
    gain1, gain2 = gain_first[None], gain_second[None]

    def prepare(block):
        return call(
            prepare_kernel,
            "prepare",
            [jax.ShapeDtypeStruct(block.shape, bf16)] * 2,
            [],
            40 * block.size,
            block,
            gain1,
        )

    near = permute(inputs, antipode)
    h1, e1 = prepare(inputs)
    folded = jnp.concatenate([project[:, :width], project[:, width:]], axis=0)
    sent_up, sent_down, sent, near = lax.optimization_barrier(
        (weight[:2], jnp.stack([weight[2], folded]), weight, near)
    )
    far = permute(near, hand_on)
    up, down = permute(sent_up, along_y(1)), permute(sent_down, along_y(-1))
    weight_s, folded_s = permute(sent, sister), permute(sent_down[1], sister)
    h0, e0 = prepare(near)
    h2, e2 = prepare(far)
    up, down, h0, h1, h2, folded_s = lax.optimization_barrier((up, down, h0, h1, h2, folded_s))
    up_s, down_s = permute(up, sister), permute(down, sister)
    pieces = (weight, folded, weight_s, folded_s, up, down, up_s, down_s)


    work = 2 * rows * channels * width
    kernels_whole = jax.ShapeDtypeStruct((4, channels, width), bf16)
    placed = call(
        place_kernel,
        "place",
        kernels_whole,
        [pltpu.SemaphoreType.DMA((4, 4))],
        work,
        where,
        *pieces[:6],
        specs=[SMEM_SPEC] + [ANY_SPEC] * 6,
    )
    whole, centre, grad2 = call(
        early_kernel,
        "early",
        [
            kernels_whole,
            jax.ShapeDtypeStruct((rows, width), f32),
            jax.ShapeDtypeStruct((rows, width), f32),
        ],
        [
            pltpu.SemaphoreType.DMA((4, 4)),
            pltpu.VMEM((2, rows, channels), bf16),
            pltpu.SemaphoreType.DMA((2,)),
        ],
        2 * work,
        where,
        h1,
        cotangent,
        placed,
        *pieces[6:],
        specs=[SMEM_SPEC] + [ANY_SPEC] * 2 + [VMEM_SPEC] + [ANY_SPEC] * 2,
        aliases={3: 0},
    )
    grad_mixed, sums = call(
        middle_kernel,
        "middle",
        [
            jax.ShapeDtypeStruct((rows, width), bf16),
            jax.ShapeDtypeStruct((16, (channels + width) // 128, 128), f32),
        ],
        [
            pltpu.VMEM((rows, width), f32),
            pltpu.VMEM((8, width), f32),
            pltpu.VMEM((rows, channels), bf16),
            pltpu.VMEM((rows, channels), bf16),
            pltpu.VMEM((rows, channels), bf16),
            pltpu.VMEM((rows, channels), bf16),
            pltpu.SemaphoreType.DMA((4,)),
        ],
        5 * work,
        h0,
        h2,
        e0,
        e1,
        e2,
        whole,
        centre,
        grad2,
        gain2,
        specs=[ANY_SPEC, VMEM_SPEC] + [ANY_SPEC] * 3 + [VMEM_SPEC] * 4,
    )
    near_grad = permute(grad_mixed, antipode)
    far_grad = permute(grad_mixed, second_neighbour)
    sums = lax.all_to_all(sums, "z", 0, 0)
    sums = call(
        spread_kernel, "spread", jax.ShapeDtypeStruct((32,) + sums.shape[1:], f32), [], 1, sums
    )
    sums = lax.all_to_all(sums, ("x", "yh", "yl", "c"), 0, 0)

    grad_input = call(
        last_kernel,
        "last",
        jax.ShapeDtypeStruct(inputs.shape, bf16),
        [pltpu.VMEM(inputs.shape, f32)],
        3 * work,
        inputs,
        cotangent,
        near_grad,
        grad_mixed,
        far_grad,
        whole,
        gain1,
    )
    lines = channels // 128
    first_sum = jnp.sum(sums[:, :lines], axis=0).reshape(-1)
    second_sum = jnp.sum(sums[:, lines:], axis=0).reshape(-1)
    return (grad_input.reshape(block_input.shape), first_sum, second_sum)


def solution(mesh):
    fine = Mesh(mesh.devices.reshape(SIZES), AXES)
    in_specs = (
        P(FSDP, SEQ, None),
        P(None, FSDP, None),
        P(FSDP, None),
        P(),
        P(),
        P(FSDP, SEQ, None),
    )
    out_specs = (P(FSDP, SEQ, None), P(), P())
    return jax.shard_map(body, mesh=fine, in_specs=in_specs, out_specs=out_specs, check_vma=False)
```

```python
import jax
import jax.numpy as jnp
import numpy as np
from jax import lax
from jax.experimental import pallas as pl
from jax.experimental.pallas import tpu as pltpu
from jax.sharding import Mesh
from jax.sharding import PartitionSpec as P

AXES = ("x", "yh", "z", "yl", "c")
SIZES = (4, 2, 16, 2, 2)
SEQ = ("x", "yh", "z")
FSDP = ("yl", "c")
HALF = 0.7978845608028654
VMEM_LIMIT = 16 * 1024 * 1024


def permute(value, target):
    pairs = []
    for place in np.ndindex(*SIZES):
        to = target(*place)
        if to is not None:
            pairs.append(
                (int(np.ravel_multi_index(place, SIZES)), int(np.ravel_multi_index(to, SIZES)))
            )
    return lax.ppermute(value, AXES, pairs)


def along_y(steps):
    def target(x, yh, z, yl, c):
        y = (2 * yh + yl + steps) % 4
        return (x, y // 2, z, y % 2, c)

    return target


def sister(x, yh, z, yl, c):
    return (x, yh, z, yl, 1 - c)


def antipode(x, yh, z, yl, c):
    return (x, 1 - yh, z, yl, c)


def hand_on(x, yh, z, yl, c):
    to = x + 1 - 2 * yh
    return (to, yh, z, yl, c) if 0 <= to < 4 else None


def second_neighbour(x, yh, z, yl, c):
    to = x + 1 - 2 * (1 - yh)
    return (to, 1 - yh, z, yl, c) if 0 <= to < 4 else None


CHUNK = 16


def normed(values):
    centre = values - jnp.mean(values, axis=-1, keepdims=True)
    spread = jnp.mean(centre * centre, axis=-1, keepdims=True)
    scale = lax.rsqrt(spread + 1e-05)
    return centre * scale, scale


def bend(a):
    square = a * a
    t = jnp.tanh(HALF * a * (1.0 + 0.044715 * square))
    return t, 0.5 * (1.0 + t) + (0.5 * HALF) * a * (1.0 - t * t) * (1.0 + 0.134145 * square)


def norm_back(grad, scale, unit):
    return scale * (
        grad
        - jnp.mean(grad, axis=-1, keepdims=True)
        - unit * jnp.mean(grad * unit, axis=-1, keepdims=True)
    )


def over_rows(count, step):
    def run(i, carry):
        step(pl.ds(pl.multiple_of(i * CHUNK, CHUNK), CHUNK))
        return carry

    lax.fori_loop(0, count // CHUNK, run, 0, unroll=True)


def prepare_kernel(block, gain, hidden, weigh):
    def step(rows):
        unit, scale = normed(block[rows, :].astype(jnp.float32))
        a = unit * gain[...]
        t, slope = bend(a)
        hidden[rows, :] = (0.5 * a * (1.0 + t)).astype(jnp.bfloat16)
        weigh[rows, :] = slope * unit

    over_rows(block.shape[0], step)


def gather(where, pieces, whole, semaphores, slabs, shards):
    copies = {}
    for k in slabs:
        for r in shards:
            ref, slab = pieces[r][k]
            part = ref.shape[-2]
            place = pl.ds(pl.multiple_of(where[r], 128), part)
            copies[k, r] = pltpu.make_async_copy(
                ref.at[slab] if slab is not None else ref,
                whole.at[k ^ where[4] if k in (0, 2) else k, place],
                semaphores.at[k, r],
            )
            copies[k, r].start()

    def ready(k):
        for r in shards:
            copies[k, r].wait()

    return ready


def place_kernel(where, weight, folded, weight_s, folded_s, up, down, whole, semaphores):
    pieces = [
        [(weight, 0), (weight, 1), (weight, 2), (folded, None)],
        [(weight_s, 0), (weight_s, 1), (weight_s, 2), (folded_s, None)],
        [(up, 0), (up, 1), (down, 0), (down, 1)],
    ]
    ready = gather(where, pieces, whole, semaphores, range(4), range(3))
    for k in range(4):
        ready(k)


def fetch(sources, places, semaphores):
    copies = [
        pltpu.make_async_copy(source, place, semaphores.at[i])
        for i, (source, place) in enumerate(zip(sources, places))
    ]
    for copy in copies:
        copy.start()
    return lambda i: copies[i].wait()


def early_kernel(
    where, hidden_away, cotangent_away, placed, up_s, down_s, whole, mixed, grad2, semaphores,
    held_rows, row_semaphores,
):
    hidden, cotangent = held_rows.at[0], held_rows.at[1]
    fetched = fetch((hidden_away, cotangent_away), (hidden, cotangent), row_semaphores)
    fourth = [(up_s, 0), (up_s, 1), (down_s, 0), (down_s, 1)]
    ready = gather(where, {3: fourth}, whole, semaphores, (3, 1, 0, 2), (3,))
    width = mixed.shape[1]
    half = whole.shape[1] // 8

    ready(3)
    fetched(1)
    for j in range(2):
        held = jnp.concatenate(
            [whole[3, (2 * f + j) * half : (2 * f + j + 1) * half, :] for f in range(4)], axis=0
        )
        product = dot_t(cotangent[:, j * width : (j + 1) * width], held)
        grad2[...] = product if j == 0 else grad2[...] + product
    ready(1)
    fetched(0)
    mixed[...] = dot(hidden[...], whole[1])
    ready(0)
    ready(2)


def middle_kernel(
    h0_away, h2, e0_away, e1_away, e2_away, whole, centre, grad2, gain, grad_mixed, sums, mixed,
    partial, h0, e0, e1, e2, semaphores,
):
    fetched = fetch((h0_away, e0_away, e1_away, e2_away), (h0, e0, e1, e2), semaphores)
    rows, width = mixed.shape
    channels = e0.shape[1]
    for n in range(0, width, 256):
        cols = slice(n, n + 256)
        mixed[:, cols] = centre[:, cols] + dot(h2[...], whole[2, :, cols])
    fetched(0)
    for n in range(0, width, 256):
        cols = slice(n, n + 256)
        mixed[:, cols] += dot(h0[...], whole[0, :, cols])
    partial[...] = jnp.zeros_like(partial)

    def step(at):
        unit, scale = normed(mixed[at, :].astype(jnp.bfloat16).astype(jnp.float32))
        unused, slope = bend(unit * gain[...])
        grad_a = grad2[at, :] * slope
        terms = grad_a * unit
        partial[...] += jnp.sum(terms.reshape(-1, 8, width), axis=0)
        grad_mixed[at, :] = norm_back(grad_a * gain[...], scale, unit).astype(jnp.bfloat16)

    over_rows(rows, step)

    def put(start, row):
        for i in range(0, row.shape[1], 128):
            j = (start + i) // 128
            sums[:, j : j + 1, :] = jnp.broadcast_to(
                row[:, i : i + 128][None], (sums.shape[0], 1, 128)
            )

    for i in range(1, 4):
        fetched(i)
    put(channels, jnp.sum(partial[...], axis=0, keepdims=True))
    for n in range(0, channels, 256):
        cols = slice(n, n + 256)
        terms = dot_t(grad_mixed[...], whole[0, cols, :]) * e0[:, cols]
        terms += dot_t(grad_mixed[...], whole[1, cols, :]) * e1[:, cols]
        terms += dot_t(grad_mixed[...], whole[2, cols, :]) * e2[:, cols]
        put(n, jnp.sum(terms, axis=0, keepdims=True))


def spread_kernel(arrived, sums):
    total = jnp.sum(arrived[...], axis=0, keepdims=True)
    sums[...] = jnp.broadcast_to(total, sums.shape)


def last_kernel(
    block, cotangent, near, here, far, away, gain, result, grads, whole, semaphores
):
    fetched = fetch(
        [away.at[k] for k in (1, 2, 0)], [whole.at[k] for k in (1, 2, 0)], semaphores
    )
    rows, channels = block.shape
    for i, (k, grad) in enumerate(((1, here), (2, near), (0, far))):
        fetched(i)
        for n in range(0, channels, 256):
            cols = slice(n, n + 256)
            product = dot_t(grad[...], whole[k, cols, :])
            grads[:, cols] = product if i == 0 else grads[:, cols] + product

    def step(at):
        unit, scale = normed(block[at, :].astype(jnp.float32))
        unused, slope = bend(unit * gain[...])
        branch = norm_back(grads[at, :] * slope * gain[...], scale, unit)
        result[at, :] = (cotangent[at, :].astype(jnp.float32) + branch).astype(jnp.bfloat16)

    over_rows(rows, step)


VMEM_SPEC = pl.BlockSpec(memory_space=pltpu.VMEM)
SMEM_SPEC = pl.BlockSpec(memory_space=pltpu.SMEM)
ANY_SPEC = pl.BlockSpec(memory_space=pl.ANY)
HBM_SPEC = pl.BlockSpec(memory_space=pltpu.HBM)


def call(kernel, name, out_shape, scratch, flops, *operands, specs=None, aliases=None):
    moved = sum(v.size * v.dtype.itemsize for v in operands)
    return pl.pallas_call(
        kernel,
        name=name,
        out_shape=out_shape,
        in_specs=specs or [VMEM_SPEC] * len(operands),
        out_specs=jax.tree.map(lambda _: VMEM_SPEC, out_shape),
        scratch_shapes=scratch,
        input_output_aliases=aliases or {},
        cost_estimate=pl.CostEstimate(flops=flops, bytes_accessed=moved, transcendentals=0),
        compiler_params=pltpu.CompilerParams(vmem_limit_bytes=VMEM_LIMIT),
    )(*operands)


def dot(a, b):
    return lax.dot_general(a, b, (((1,), (0,)), ((), ())), preferred_element_type=jnp.float32)


def dot_t(a, b):
    return lax.dot_general(a, b, (((1,), (1,)), ((), ())), preferred_element_type=jnp.float32)


def body(block_input, weight, project, gain_first, gain_second, grad_output):
    samples, bins, channels = block_input.shape
    rows = samples * bins
    width = weight.shape[2]
    part = weight.shape[1]
    part_h = project.shape[0]
    inputs = block_input.reshape(rows, channels)
    cotangent = grad_output.reshape(rows, channels)

    own = lax.axis_index(FSDP)
    where = jnp.stack([(own ^ r) * part for r in range(4)] + [2 - 2 * lax.axis_index("yh")])

    f32, bf16 = jnp.float32, jnp.bfloat16
    gain1, gain2 = gain_first[None], gain_second[None]

    def prepare(block):
        return call(
            prepare_kernel,
            "prepare",
            [jax.ShapeDtypeStruct(block.shape, bf16), jax.ShapeDtypeStruct(block.shape, f32)],
            [],
            40 * block.size,
            block,
            gain1,
        )

    near = permute(inputs, antipode)
    h1, e1 = prepare(inputs)
    folded = jnp.concatenate([project[:, :width], project[:, width:]], axis=0)
    sent_up, sent_down, sent, near = lax.optimization_barrier(
        (weight[:2], jnp.stack([weight[2], folded]), weight, near)
    )
    far = permute(near, hand_on)
    up, down = permute(sent_up, along_y(1)), permute(sent_down, along_y(-1))
    weight_s, folded_s = permute(sent, sister), permute(sent_down[1], sister)
    h0, e0 = prepare(near)
    h2, e2 = prepare(far)
    up, down, h0, h1, h2, folded_s = lax.optimization_barrier((up, down, h0, h1, h2, folded_s))
    up_s, down_s = permute(up, sister), permute(down, sister)
    pieces = (weight, folded, weight_s, folded_s, up, down, up_s, down_s)


    work = 2 * rows * channels * width
    kernels_whole = jax.ShapeDtypeStruct((4, channels, width), bf16)
    placed = call(
        place_kernel,
        "place",
        kernels_whole,
        [pltpu.SemaphoreType.DMA((4, 4))],
        work,
        where,
        *pieces[:6],
        specs=[SMEM_SPEC] + [HBM_SPEC] * 6,
    )
    whole, centre, grad2 = call(
        early_kernel,
        "early",
        [
            kernels_whole,
            jax.ShapeDtypeStruct((rows, width), f32),
            jax.ShapeDtypeStruct((rows, width), f32),
        ],
        [
            pltpu.SemaphoreType.DMA((4, 4)),
            pltpu.VMEM((2, rows, channels), bf16),
            pltpu.SemaphoreType.DMA((2,)),
        ],
        2 * work,
        where,
        h1,
        cotangent,
        placed,
        *pieces[6:],
        specs=[SMEM_SPEC] + [HBM_SPEC] * 2 + [VMEM_SPEC] + [HBM_SPEC] * 2,
        aliases={3: 0},
    )
    grad_mixed, sums = call(
        middle_kernel,
        "middle",
        [
            jax.ShapeDtypeStruct((rows, width), bf16),
            jax.ShapeDtypeStruct((16, (channels + width) // 128, 128), f32),
        ],
        [
            pltpu.VMEM((rows, width), f32),
            pltpu.VMEM((8, width), f32),
            pltpu.VMEM((rows, channels), bf16),
            pltpu.VMEM((rows, channels), f32),
            pltpu.VMEM((rows, channels), f32),
            pltpu.VMEM((rows, channels), f32),
            pltpu.SemaphoreType.DMA((4,)),
        ],
        5 * work,
        h0,
        h2,
        e0,
        e1,
        e2,
        whole,
        centre,
        grad2,
        gain2,
        specs=[HBM_SPEC, VMEM_SPEC] + [HBM_SPEC] * 3 + [VMEM_SPEC] * 4,
    )
    near_grad = permute(grad_mixed, antipode)
    far_grad = permute(grad_mixed, second_neighbour)
    sums = lax.all_to_all(sums, "z", 0, 0)
    sums = call(
        spread_kernel, "spread", jax.ShapeDtypeStruct((32,) + sums.shape[1:], f32), [], 1, sums
    )
    sums = lax.all_to_all(sums, ("x", "yh", "yl", "c"), 0, 0)

    grad_input = call(
        last_kernel,
        "last",
        jax.ShapeDtypeStruct(inputs.shape, bf16),
        [
            pltpu.VMEM(inputs.shape, f32),
            pltpu.VMEM((3, channels, width), bf16),
            pltpu.SemaphoreType.DMA((3,)),
        ],
        3 * work,
        inputs,
        cotangent,
        near_grad,
        grad_mixed,
        far_grad,
        whole,
        gain1,
        specs=[VMEM_SPEC] * 5 + [HBM_SPEC, VMEM_SPEC],
    )
    lines = channels // 128
    first_sum = jnp.sum(sums[:, :lines], axis=0).reshape(-1)
    second_sum = jnp.sum(sums[:, lines:], axis=0).reshape(-1)
    return (grad_input.reshape(block_input.shape), first_sum, second_sum)


def solution(mesh):
    fine = Mesh(mesh.devices.reshape(SIZES), AXES)
    in_specs = (
        P(FSDP, SEQ, None),
        P(None, FSDP, None),
        P(FSDP, None),
        P(),
        P(),
        P(FSDP, SEQ, None),
    )
    out_specs = (P(FSDP, SEQ, None), P(), P())
    return jax.shard_map(body, mesh=fine, in_specs=in_specs, out_specs=out_specs, check_vma=False)
```
